128 devices in a mesh: lat: 4 (over z_lo, core), lon: 32 (over y, x, z_hi).
Axes of the slice: x: 4, y: 4, z: 4 (z_hi: 2, z_lo: 2; z = z_hi * 2 + z_lo), core: 2. Of those that a mesh axis runs over, the one named last changes fastest.
Arguments:
- tracers: float32 [4, 32, 128, 4096], P(None, None, 'lat', 'lon'), may hold values from -6 to 6
- vel_east: float32 [32, 128, 4096], P(None, 'lat', 'lon'), may hold values from -0.18 to 0.18
- vel_north: float32 [32, 128, 4096], P(None, 'lat', 'lon'), may hold values from -0.18 to 0.18
- land_mask: int32 [32, 128, 4096], P(None, 'lat', 'lon'), may hold values 0 or 1
- step_area: float32 [128, 4096], P('lat', 'lon'), may hold values from 1.5 to 4
- float_cell: int32 [32768], P(('lat', 'lon')), may hold values from 0 to 4095
- float_owner: int32 [32768, 1], P(('lat', 'lon')), may hold values from 0 to 127; in each aligned block of 256 rows (0 to 255, 256 to 511, ...) at most 4 rows name the same one
Outputs:
- tracers_out: float32 [4, 32, 128, 4096], P(None, None, 'lat', 'lon')
- arrivals: float32 [65536, 128], P(('lat', 'lon'))
- arrival_counts: int32 [16384], P(('lat', 'lon'))
The draws below stay inside these ranges and needn't reach their ends.
Inputs may be any that keep to these rules, and one draw needn't show every extreme that they name: `float_owner`: among the 256 rows of one device no device number appears more than 4 times, and in some device's rows one appears exactly 4 times.
All inputs are finite; a program needn't handle non-finite values. No bound on the sum of `land_mask` on one device may be relied on, other than what follows from the above.
Results may differ from the reference program's by a relative error of at most 0.0003.
Values sent between devices are 32-bit elements; how exact they have to be, the bound alone decides.
No kernel may reach another device: no remote copies, remote signals or barrier semaphores. Data moves between devices by JAX's collectives and lax.ppermute only.
A program may use at most 128 MiB of HBM per device.

```python
import math
import jax
import jax.numpy as jnp
import numpy as np
from jax import lax

TRACERS = 4
LEV = 32
CLAT = 32
CLON = 128
CAP = 4
FLT_DEV = 256
FLOATS = 32768
RECW = 128
NLAT = 128
NLON = 4096
N_LON = 32
DEVICES = 128


def draw_tracers(key, part):
    base_key = jax.random.fold_in(key, 11)
    key_body, key_sign, key_size = jax.random.split(base_key, 3)
    grid_shape = (TRACERS, LEV, NLAT, NLON)
    row_local = jnp.arange(NLAT, dtype=jnp.int32) % CLAT
    col_local = jnp.arange(NLON, dtype=jnp.int32) % CLON
    row_edge = (row_local == 2) | (row_local == 3) | (row_local == CLAT - 3) | (row_local == CLAT - 4)
    col_edge = (col_local == 2) | (col_local == 3) | (col_local == CLON - 3) | (col_local == CLON - 4)
    near_edge = row_edge[:, None] | col_edge[None, :]
    flip_sign = jnp.where(jax.random.bernoulli(key_sign, 0.5, grid_shape), 1.0, -1.0).astype(jnp.float32)
    inner_values = jnp.clip(jax.random.normal(key_body, grid_shape, jnp.float32), -4.0, 4.0)
    edge_size = jax.random.uniform(key_size, grid_shape, jnp.float32, 4.0, 6.0)
    return jnp.where(near_edge[None, None], flip_sign * edge_size, inner_values).astype(jnp.float32)


def flow_field(key, salt, along_rows):
    base_key = jax.random.fold_in(key, salt)
    key_sign, key_size = jax.random.split(base_key, 2)
    grid_shape = (LEV, NLAT, NLON)
    if along_rows:
        sign_shape = (LEV, NLAT, 1)
    else:
        sign_shape = (LEV, 1, NLON)
    flip_sign = jnp.where(jax.random.bernoulli(key_sign, 0.5, sign_shape), 1.0, -1.0).astype(jnp.float32)
    magnitude = jax.random.uniform(key_size, grid_shape, jnp.float32, 0.12, 0.18)
    return (flip_sign * magnitude).astype(jnp.float32)


def draw_vel_east(key, part):
    return flow_field(key, 23, True)


def draw_vel_north(key, part):
    return flow_field(key, 37, False)


def set_ends(drawn, key, smallest, largest):
    index_at = [jax.random.randint(jax.random.fold_in(key, axis), (), 0, length) for axis, length in enumerate(drawn.shape)]
    main_axis = drawn.shape.index(max(drawn.shape))
    beside = index_at[:main_axis] + [(index_at[main_axis] + 1) % drawn.shape[main_axis]] + index_at[main_axis + 1:]
    return drawn.at[tuple(index_at)].set(smallest).at[tuple(beside)].set(largest)


def shard_levels(rng, dims, cuts, smallest, high):
    factor_of = 1.0
    for axis_at, shards_of in cuts:
        heights = jax.random.uniform(jax.random.fold_in(jax.random.fold_in(rng, 6), axis_at), (shards_of,), jnp.float32, smallest / len(cuts), high / len(cuts))
        factor_of = factor_of * jnp.repeat(jnp.exp(heights), dims[axis_at] // shards_of).reshape((-1,) + (1,) * (len(dims) - 1 - axis_at))
    return factor_of


def assign_block(own_key, own, number, rows, number_of, top, bound, skew):
    order = jax.random.permutation(own_key, number_of)
    heavy_load, ordinary = load_shares(number_of, rows * top, bound, skew, True), load_shares(number_of, rows * top, bound, skew, False)
    places = jnp.arange(number_of)

    def named(tallies, offset_by):
        used = int((tallies > 0).sum())
        fixed = max(1, used // 4)
        passed = fixed + (places - fixed + offset_by * (used - fixed)) % max(1, number_of - fixed)
        return jnp.zeros((number_of,), jnp.int32).at[order[jnp.where(places < fixed, places, passed)]].set(jnp.asarray(tallies, jnp.int32))

    tallies = jnp.where(number % 4 == 0, named(heavy_load, number // 4), named(ordinary, number - number // 4 - 1))
    mixed = jax.random.permutation(jax.random.fold_in(own, 3), number_of)
    giver, receiver = mixed[0:number_of // 2 * 2:2], mixed[1:number_of // 2 * 2:2]
    slack = jnp.minimum(tallies[giver] - 1, bound - tallies[receiver]) // 2
    slack = jnp.where((giver == order[0]) | (receiver == order[0]) | (tallies[receiver] == 0), 0, jnp.maximum(slack, 0))
    passed = jax.random.randint(jax.random.fold_in(own, 4), (number_of // 2,), 0, 1 << 20) % (slack + 1)
    tallies = tallies.at[giver].add(-passed).at[receiver].add(passed)
    items = jnp.searchsorted(jnp.cumsum(tallies), jnp.arange(rows * top), side="right").astype(jnp.int32)
    listing = items.reshape(top, rows).T
    listing = listing[jax.random.permutation(jax.random.fold_in(own, 1), rows)]
    offset_by = jax.random.randint(jax.random.fold_in(own, 2), (rows, 1), 0, top)
    return jnp.take_along_axis(listing, (jnp.arange(top)[None, :] + offset_by) % top, axis=1)


def load_shares(amount, total, most, skew, full):
    loads = [(1 << 20) // math.isqrt(rank ** skew) + 1 for rank in range(1, amount + 1)]
    largest = most if full else min(most, max(-(-total // amount), total * loads[0] // sum(loads)))
    least = 1 if total - largest >= amount - 1 else 0
    holding, rest = [largest] + [least] * (amount - 1), total - largest - least * (amount - 1)
    while rest > 0:
        candidates = [i for i in range(1, amount) if holding[i] < largest] or [i for i in range(1, amount) if holding[i] < most]
        mass, left = sum([loads[i] for i in candidates]), rest
        for i in candidates:
            extra = min(most - holding[i], max(1, left * loads[i] // mass), rest)
            holding[i] = holding[i] + extra
            rest = rest - extra
    return np.array(holding)


def setup_inputs(seed: int = 0) -> dict:
    splits = jax.random.split(jax.random.key(seed), 8)
    tracers = draw_tracers(jax.random.fold_in(splits[7], 71), 0)
    vel_east = draw_vel_east(jax.random.fold_in(splits[7], 71), 0)
    vel_north = draw_vel_north(jax.random.fold_in(splits[7], 71), 0)
    land_mask = set_ends((jax.random.randint(splits[3], (LEV, NLAT, NLON), 0, 8) < 7).astype(jnp.int32), jax.random.fold_in(splits[3], 1), 0, 1)
    step_area = jnp.clip(jnp.exp(math.log(4.0) - 0.98082925 * jax.random.uniform(splits[4], (NLAT, NLON), jnp.float32) ** shard_levels(splits[4], (NLAT, NLON), ((0, 4), (1, 32)), -0.2, 0.2)), 1.5, 4.0)
    float_cell = set_ends(jax.random.randint(splits[5], (FLOATS,), 0, CLAT * CLON), jax.random.fold_in(splits[5], 1), 0, (CLAT * CLON) - 1).astype(jnp.int32)
    float_owner_keys = jax.random.split(jax.random.fold_in(splits[6], 1), FLOATS // FLT_DEV)
    float_owner_turns = jax.random.permutation(jax.random.fold_in(splits[6], 3), FLOATS // FLT_DEV)
    float_owner = jax.vmap(lambda own, number: assign_block(jax.random.fold_in(splits[6], 2), own, number, FLT_DEV, DEVICES, 1, CAP, 2))(float_owner_keys, float_owner_turns).reshape((FLOATS, 1))
    return {"tracers": tracers, "vel_east": vel_east, "vel_north": vel_north, "land_mask": land_mask, "step_area": step_area, "float_cell": float_cell, "float_owner": float_owner}


def face_flux(velocity, behind, current, forward, farther):
    return velocity * (7.0 * (current + forward) - (behind + farther)) / 12.0 - jnp.abs(velocity) * (3.0 * (forward - current) - (farther - behind)) / 12.0


def advance(tracer_pad, static_pad, step_area, row_count, col_count):
    flow_east, flow_north, wet_pad = static_pad[0], static_pad[1], static_pad[2]
    lon_strip = tracer_pad[..., 2:row_count + 2, :]
    open_east = flow_east[:, 2:row_count + 2, 1:col_count + 2] * wet_pad[:, 2:row_count + 2, 1:col_count + 2] * wet_pad[:, 2:row_count + 2, 2:col_count + 3]
    flux_x = face_flux(open_east, lon_strip[..., 0:col_count + 1], lon_strip[..., 1:col_count + 2], lon_strip[..., 2:col_count + 3], lon_strip[..., 3:col_count + 4])
    lat_strip = tracer_pad[..., 2:col_count + 2]
    open_north = flow_north[:, 1:row_count + 2, 2:col_count + 2] * wet_pad[:, 1:row_count + 2, 2:col_count + 2] * wet_pad[:, 2:row_count + 3, 2:col_count + 2]
    flux_y = face_flux(open_north, lat_strip[..., 0:row_count + 1, :], lat_strip[..., 1:row_count + 2, :], lat_strip[..., 2:row_count + 3, :], lat_strip[..., 3:row_count + 4, :])
    change = (flux_x[..., 1:] - flux_x[..., :-1]) + (flux_y[..., 1:, :] - flux_y[..., :-1, :])
    centre = tracer_pad[..., 2:row_count + 2, 2:col_count + 2]
    return centre - step_area * wet_pad[:, 2:row_count + 2, 2:col_count + 2] * change


def extend(field_in, folded):
    fold_rows = jnp.flip(field_in[..., NLAT - 2:, :], axis=(-2, -1))
    if not folded:
        fold_rows = jnp.zeros_like(fold_rows)
    low_rows = jnp.zeros_like(field_in[..., :2, :])
    lat_padded = jnp.concatenate([low_rows, field_in, fold_rows], axis=-2)
    return jnp.concatenate([lat_padded[..., -2:], lat_padded, lat_padded[..., :2]], axis=-1)


def reference(tracers, vel_east, vel_north, land_mask, step_area, float_cell, float_owner):
    wet_mask = land_mask.astype(jnp.float32)
    static_pad = jnp.stack([extend(vel_east, False), extend(vel_north, False), extend(wet_mask, True)])

    def advect_one(single):
        after_one = advance(extend(single, True), static_pad, step_area, NLAT, NLON)
        return advance(extend(after_one, True), static_pad, step_area, NLAT, NLON)

    finished = lax.map(advect_one, tracers)
    row_index = jnp.arange(FLOATS, dtype=jnp.int32)
    source = row_index // FLT_DEV
    band_index = source // N_LON
    slab_index = source % N_LON
    grid_lat = band_index * CLAT + float_cell // CLON
    grid_lon = slab_index * CLON + float_cell % CLON
    samples = finished[:, :, grid_lat, grid_lon]
    records = jnp.transpose(samples, (2, 0, 1)).reshape(FLOATS, RECW)
    owner = float_owner[:, 0]
    blocks = owner.reshape(DEVICES, FLT_DEV)
    local_index = jnp.arange(FLT_DEV, dtype=jnp.int32)
    earlier = local_index[None, :] < local_index[:, None]
    same_owner = (blocks[:, :, None] == blocks[:, None, :]) & earlier[None]
    slot_rank = jnp.sum(same_owner.astype(jnp.int32), axis=2).reshape(FLOATS)
    slot_index = owner * (DEVICES * CAP) + source * CAP + slot_rank
    arrivals = jnp.zeros((DEVICES * DEVICES * CAP, RECW), jnp.float32).at[slot_index].set(records)
    arrival_counts = jnp.zeros((DEVICES * DEVICES,), jnp.int32).at[owner * DEVICES + source].add(jnp.ones((FLOATS,), jnp.int32))
    return finished, arrivals, arrival_counts
```

```python
import jax
import jax.numpy as jnp
from jax import lax
from jax.experimental import pallas as pl
from jax.experimental.pallas import tpu as pltpu
from jax.sharding import PartitionSpec as P

CAP = 4
NT, LEV, ROWS, COLS = 4, 32, 32, 128
KG = LEV // 8
SLOTS = 24
S_VE, S_VN, S_M = 16, 18, 21
QUADS = 9
ABSENT = 1e30


def lanes():
    return lax.broadcasted_iota(jnp.int32, (8, COLS), 1)


def pick(x, index):
    return jnp.take_along_axis(x, index, axis=1, mode="promise_in_bounds")


def full(shape, dtype=jnp.float32):
    return jax.ShapeDtypeStruct(shape, dtype)


def params():
    return pltpu.CompilerParams(vmem_limit_bytes=56 * 1024 * 1024)


def vmem():
    return pl.BlockSpec(memory_space=pltpu.VMEM)


def rows_kernel(q_lo, q_hi, ve_lo, ve_hi, vn_lo, vn_hi, lm_lo, lm_hi, area, out_p, out_q):
    lat = lax.axis_index("lat")
    even = lat % 2 == 0
    fold = lat == 3
    flip = COLS - 1 - lanes()

    def take(ref, plane, row):
        return ref[pl.ds(plane * 8 + row, 8, stride=8), :]

    def mass(ref, kg, row, at):
        wet = take(ref, kg * 8, row).astype(jnp.float32)
        return wet * jnp.broadcast_to(area[at : at + 1, :], (8, COLS))

    for kg in range(KG):

        def put(slot, bottom, normal, mirrored):
            top = jnp.where(fold, pick(mirrored, flip), normal)
            out_p[slot, kg * 8 : kg * 8 + 8, :] = jnp.where(even, top, bottom)
            out_q[slot, kg * 8 : kg * 8 + 8, :] = jnp.where(even, bottom, top)

        for c in range(NT):
            plane = c * LEV + kg * 8
            low = [take(q_lo, plane, r) for r in range(4)]
            high = [take(q_hi, plane, 4 + r) for r in range(4)]
            for r in range(4):
                put(c * 4 + r, low[r], high[r], high[3 - r])
        low = [take(ve_lo, kg * 8, r) for r in range(2)]
        high = [take(ve_hi, kg * 8, 6 + r) for r in range(2)]
        for r in range(2):
            put(S_VE + r, low[r], high[r], -high[1 - r])
        low = [take(vn_lo, kg * 8, r) for r in (0, 0, 1)]
        high = [take(vn_hi, kg * 8, 5 + r) for r in range(3)]
        for r in range(3):
            put(S_VN + r, low[r], high[r], -high[2 - r])
        low = [mass(lm_lo, kg, r, r) for r in range(3)]
        high = [mass(lm_hi, kg, 5 + r, 29 + r) for r in range(3)]
        for r in range(3):
            put(S_M + r, low[r], high[r], high[2 - r])


def pack_rows(tracers, ve, vn, lm, area):
    def edge(array, last):
        n = array.shape[0]
        block = array.reshape(n, ROWS // 8, 8, COLS)[:, 3 if last else 0]
        return block.reshape(n * 8, COLS)

    def spec(n, at):
        return pl.BlockSpec((n, 8, COLS), lambda i: (0, at, 0))

    def body(*refs):
        refs = list(refs)
        flat = [r.reshape(r.shape[0] * 8, COLS) for r in refs[:8]]
        rows_kernel(*flat, *refs[8:])

    q3 = tracers.reshape(NT * LEV, ROWS, COLS)
    return pl.pallas_call(
        body,
        grid=(1,),
        in_specs=[
            spec(NT * LEV, 0), spec(NT * LEV, 3), spec(LEV, 0), spec(LEV, 3),
            spec(LEV, 0), spec(LEV, 3), spec(LEV, 0), spec(LEV, 3),
            pl.BlockSpec((ROWS, COLS), lambda i: (0, 0)),
        ],
        out_specs=[pl.BlockSpec((SLOTS, LEV, COLS), lambda i: (0, 0, 0))] * 2,
        out_shape=[full((SLOTS, LEV, COLS))] * 2,
        compiler_params=params(),
        name="pack_rows",
    )(q3, q3, ve, ve, vn, vn, lm, lm, area)


class Band:
    def __init__(self, q, ve, vn, lm, area, in_p, in_q):
        self.q, self.ve, self.vn, self.lm, self.area = q, ve, vn, lm, area
        self.in_p, self.in_q = in_p, in_q
        self.even = lax.axis_index("lat") % 2 == 0

    def ghost(self, north, slot, kg):
        a = self.in_p[slot, kg * 8 : kg * 8 + 8, :]
        b = self.in_q[slot, kg * 8 : kg * 8 + 8, :]
        return jnp.where(self.even, a, b) if north else jnp.where(self.even, b, a)

    def own(self, ref, plane, row):
        return ref[pl.ds(plane * ROWS + row, 8, stride=ROWS), :]

    def tracer(self, c, kg, row):
        if row < 0:
            return self.ghost(False, c * 4 + row + 4, kg)
        if row >= ROWS:
            return self.ghost(True, c * 4 + row - ROWS, kg)
        return self.own(self.q, c * LEV + kg * 8, row)

    def east(self, kg, row):
        if row < 0:
            return self.ghost(False, S_VE + row + 2, kg)
        if row >= ROWS:
            return self.ghost(True, S_VE + row - ROWS, kg)
        return self.own(self.ve, kg * 8, row)

    def north(self, kg, face):
        if face < 0:
            return self.ghost(False, S_VN + face + 3, kg)
        if face >= ROWS:
            return self.ghost(True, S_VN + 1 + face - ROWS, kg)
        return self.own(self.vn, kg * 8, face)

    def mass(self, kg, row):
        if row < 0:
            return self.ghost(False, S_M + row + 3, kg)
        if row >= ROWS:
            return self.ghost(True, S_M + row - ROWS, kg)
        wet = self.own(self.lm, kg * 8, row).astype(jnp.float32)
        return wet * jnp.broadcast_to(self.area[row : row + 1, :], (8, COLS))

    def fields(self, kg, row):
        return [self.tracer(c, kg, row) for c in range(NT)] + [
            self.east(kg, row), self.north(kg, row), self.mass(kg, row)
        ]


def quad_rows(quad):
    return [-2, -1, ROWS, ROWS + 1] if quad == QUADS - 1 else [quad * 4 + r for r in range(4)]


def cols_kernel(q, ve, vn, lm, area, in_p, in_q, out_r, out_s):
    band = Band(q, ve, vn, lm, area, in_p, in_q)
    even = lax.axis_index("lon") % 2 == 0
    lane = lanes()
    ends = jnp.where(lane < 64, lane % 4, COLS - 4 + lane % 4)
    place = (lane % 64) // 4
    for quad in range(QUADS):
        for kg in range(KG):
            halves = []
            for pair in range(2):
                acc = jnp.zeros((8, COLS), jnp.float32)
                for h in range(2):
                    for f, x in enumerate(band.fields(kg, quad_rows(quad)[pair * 2 + h])):
                        acc = jnp.where(place == 8 * h + f, pick(x, ends), acc)
                halves.append(acc)
            west = jnp.where(lane < 64, halves[0], pltpu.roll(halves[1], 64, 1))
            east = jnp.where(lane < 64, pltpu.roll(halves[0], 64, 1), halves[1])
            out_r[quad, kg * 8 : kg * 8 + 8, :] = jnp.where(even, east, west)
            out_s[quad, kg * 8 : kg * 8 + 8, :] = jnp.where(even, west, east)


def pack_cols(q, ve, vn, lm, area, in_p, in_q):
    return pl.pallas_call(
        cols_kernel,
        out_shape=[full((QUADS, LEV, COLS))] * 2,
        compiler_params=params(),
        name="pack_cols",
    )(q, ve, vn, lm, area, in_p, in_q)


ROW_LO, ROW_HI = -4, 36
SIXTH = 1.0 / 6.0


def along_columns(e, w):
    right = pltpu.roll(e, COLS - 1, 1)
    triple = 3.0 * e
    both = e + right
    behind = triple - pltpu.roll(e, 1, 1)
    ahead = pltpu.roll(triple - right, COLS - 1, 1)
    flux = w * (both + both + jnp.where(w > 0, behind, ahead))
    return flux - pltpu.roll(flux, 1, 1)


def along_rows(a, b, c, d, w):
    both = b + c
    return w * (both + both + jnp.where(w > 0, 3.0 * b - a, 3.0 * c - d))


def advance_kernel(q, ve, vn, lm, area, in_p, in_q, in_r, in_s, cell, slot, out, outbox,
                   qs, se, sn, sm, done, flat):
    band = Band(q, ve, vn, lm, area, in_p, in_q)
    lat = lax.axis_index("lat")
    fold = lat == 3
    even = lax.axis_index("lon") % 2 == 0
    lane = lanes()
    spot = lane % 32
    group = lane // 32
    own_cols = jnp.where((spot >= 4) & (spot < 12), spot - 4, jnp.where((spot >= 12) & (spot < 20), spot + 108, 0))
    low_halo = spot < 4
    high_halo = (spot >= 20) & (spot < 24)
    halo_at = jnp.where(low_halo, spot, jnp.where(high_halo, spot - 20, 0))

    def strip_of_tracers(parts):
        x = [pick(p, own_cols) for p in parts]
        return jnp.where(group < 2, jnp.where(group == 0, x[0], x[1]), jnp.where(group == 2, x[2], x[3]))

    def with_halo(x, west, east, index):
        return jnp.where(low_halo, pick(west, index), jnp.where(high_halo, pick(east, index), x))

    for kg in range(KG):
        ks = slice(kg * 8, kg * 8 + 8)
        raw = {}
        for row in range(ROW_LO, ROW_HI):
            parts = [band.tracer(c, kg, row) for c in range(NT)]
            for c in range(NT):
                qs[c, row - ROW_LO, ks, :] = parts[c]
            strip = strip_of_tracers(parts)
            main = {}
            edge = {}
            if -2 <= row < ROWS + 2:
                main["e"] = band.east(kg, row)
            if -3 <= row < ROWS + 2:
                main["n"] = band.north(kg, row)
            if -3 <= row < ROWS + 3:
                main["m"] = band.mass(kg, row)
            for name, x in main.items():
                edge[name] = pick(x, own_cols)
            if -2 <= row < ROWS + 2:
                if 0 <= row < ROWS:
                    quad, rq = row // 4, row % 4
                else:
                    quad, rq = QUADS - 1, (row + 2 if row < 0 else row - ROWS + 2)
                r_in = in_r[quad, ks, :]
                s_in = in_s[quad, ks, :]
                west = jnp.where(even, s_in, r_in)
                east = jnp.where(even, r_in, s_in)
                strip = with_halo(strip, west, east, 32 * rq + 4 * group + halo_at)
                for f, name in ((4, "e"), (5, "n"), (6, "m")):
                    edge[name] = with_halo(edge[name], west, east, 32 * rq + 4 * f + halo_at)
            qs[NT, row - ROW_LO, ks, :] = strip
            raw[row] = (main, edge)
        for part in range(2):
            for row in range(-2, ROWS + 2):
                f = raw[row][part]
                v = f["e"]
                if row >= ROWS:
                    v = jnp.where(fold, pltpu.roll(v, COLS - 1, 1), v)
                open_to = jnp.minimum(f["m"], pltpu.roll(f["m"], COLS - 1, 1)) > 0
                se[part, row + 2, ks, :] = jnp.where(open_to, v * SIXTH, 0.0)
                sm[part, row + 2, ks, :] = f["m"]
            for face in range(-3, ROWS + 2):
                v = raw[face][part]["n"]
                open_to = jnp.minimum(raw[face][part]["m"], raw[face + 1][part]["m"]) > 0
                sn[part, face + 3, ks, :] = jnp.where(open_to, v * SIXTH, 0.0)
                if face == ROWS - 1:
                    other = band.ghost(True, S_VN, kg)
                    if part == 1:
                        other = pick(other, own_cols)
                    other = jnp.where(fold, other, v)
                    sn[part, ROWS + 5, ks, :] = jnp.where(open_to, other * SIXTH, 0.0)

    def column(step, _):
        t = step // KG
        base = pl.multiple_of((step % KG) * 8, 8)
        ks = pl.ds(base, 8)
        s = t // NT
        first = {}
        e = {}
        load = lambda row: qs[t, row - ROW_LO, ks, :]
        for row in range(-4, 0):
            e[row] = load(row)
        below = None
        prev = None

        def finish(row, prev_flux):
            upper = along_rows(first[row - 1], first[row], first[row + 1], first[row + 2], sn[s, row + 3, ks, :])
            if prev_flux is None:
                prev_flux = along_rows(first[row - 2], first[row - 1], first[row], first[row + 1], sn[s, row + 2, ks, :])
            change = along_columns(first[row], se[s, row + 2, ks, :]) + (upper - prev_flux)
            done[t, row, ks, :] = first[row] - sm[s, row + 2, ks, :] * change
            return upper

        for row in range(-2, ROWS + 2):
            e[row + 2] = load(row + 2)
            if below is None:
                below = along_rows(e[row - 2], e[row - 1], e[row], e[row + 1], sn[s, row + 2, ks, :])
            if row == ROWS:
                below = along_rows(e[row - 2], e[row - 1], e[row], e[row + 1], sn[s, ROWS + 5, ks, :])
            above = along_rows(e[row - 1], e[row], e[row + 1], e[row + 2], sn[s, row + 3, ks, :])
            change = along_columns(e[row], se[s, row + 2, ks, :]) + (above - below)
            first[row] = e[row] - sm[s, row + 2, ks, :] * change
            below = above
            if row - 2 >= 0:
                prev = finish(row - 2, prev)
        return 0

    lax.fori_loop(0, (NT + 1) * KG, column, 0)

    edge_cols = (lane < 4) | (lane >= COLS - 4)
    edge_at = jnp.where(lane < 4, lane + 4, jnp.where(lane >= COLS - 4, lane - (COLS - 4) + 16, 0))

    def merge(row, _):
        planes = []
        for c in range(NT):
            for kg in range(KG):
                ks = slice(kg * 8, kg * 8 + 8)
                x = jnp.where(edge_cols, pick(done[NT, row, ks, :], edge_at + 32 * c), done[c, row, ks, :])
                out[pl.ds((c * LEV + kg * 8) * ROWS + row, 8, stride=ROWS), :] = x
                planes.append(x)
        flat[pl.ds(pl.multiple_of(row * COLS, COLS), COLS), :] = jnp.concatenate(planes, axis=0).T
        return 0

    lax.fori_loop(0, ROWS, merge, 0)

    mark = jnp.where(lane == 0, ABSENT, 0.0)
    for i in range(outbox.shape[0] // 8):
        outbox[i * 8 : i * 8 + 8, :] = mark

    def send(i, _):
        for j in range(8):
            outbox[pl.ds(slot[i * 8 + j], 1), :] = flat[pl.ds(cell[i * 8 + j], 1), :]
        return 0

    lax.fori_loop(0, cell.shape[0] // 8, send, 0)


def both_steps(q, ve, vn, lm, area, in_p, in_q, in_r, in_s, cell, slot, devices):
    smem = pl.BlockSpec(memory_space=pltpu.SMEM)
    return pl.pallas_call(
        advance_kernel,
        in_specs=[vmem()] * 9 + [smem, smem],
        out_specs=[vmem()] * 2,
        out_shape=[full(q.shape), full((devices * CAP, NT * LEV))],
        scratch_shapes=[
            pltpu.VMEM((NT + 1, ROW_HI - ROW_LO, LEV, COLS), jnp.float32),
            pltpu.VMEM((2, ROWS + 4, LEV, COLS), jnp.float32),
            pltpu.VMEM((2, ROWS + 6, LEV, COLS), jnp.float32),
            pltpu.VMEM((2, ROWS + 4, LEV, COLS), jnp.float32),
            pltpu.VMEM((NT + 1, ROWS, LEV, COLS), jnp.float32),
            pltpu.VMEM((ROWS * COLS, NT * LEV), jnp.float32),
        ],
        compiler_params=params(),
        name="both_steps",
    )(q, ve, vn, lm, area, in_p, in_q, in_r, in_s, cell, slot)


def slots_kernel(column, row, out):
    n = row.shape[1]
    at = lax.broadcasted_iota(jnp.int32, (n, n), 0)
    me = lax.broadcasted_iota(jnp.int32, (n, n), 1)
    same = (jnp.broadcast_to(column[...], (n, n)) == jnp.broadcast_to(row[...], (n, n))) & (at < me)
    rank = jnp.sum(jnp.where(same, 1.0, 0.0), axis=0, keepdims=True).astype(jnp.int32)
    out[...] = row[...] * CAP + rank


def float_slots(owner):
    n = owner.shape[0]
    return pl.pallas_call(
        slots_kernel, out_shape=full((1, n), jnp.int32), compiler_params=params(), name="float_slots"
    )(owner, owner.reshape(1, n)).reshape(n)


def arrivals_kernel(inbox, out, counts):
    total = jnp.zeros((8, COLS), jnp.float32)
    sub = lax.broadcasted_iota(jnp.int32, (8, COLS), 0)
    lane = lanes()
    for i in range(inbox.shape[0] // 8):
        x = inbox[i * 8 : i * 8 + 8, :]
        here = jnp.broadcast_to(x[:, 0:1], (8, COLS)) < ABSENT * 0.5
        out[i * 8 : i * 8 + 8, :] = jnp.where(here, x, 0.0)
        total = total + jnp.where(here & (lane == (i * 8 + sub) // CAP), 1.0, 0.0)
    counts[...] = jnp.sum(total, axis=0, keepdims=True).astype(jnp.int32)


def unpack_arrivals(inbox):
    n = inbox.shape[0]
    return pl.pallas_call(
        arrivals_kernel,
        out_shape=[full(inbox.shape), full((1, n // CAP), jnp.int32)],
        compiler_params=params(),
        name="unpack_arrivals",
    )(inbox)


def local(tracers, vel_east, vel_north, land_mask, step_area, float_cell, float_owner):
    lat_n, lon_n = lax.axis_size("lat"), lax.axis_size("lon")
    axes = ("lat", "lon")

    def swap(target):
        pairs = []
        for b in range(lat_n):
            for l in range(lon_n):
                to = target(b, l)
                if to is not None:
                    pairs.append((b * lon_n + l, to[0] * lon_n + to[1]))
        return lambda x: lax.ppermute(x, axes, pairs)

    swap_p = swap(lambda b, l: (b ^ 1, l))
    swap_q = swap(lambda b, l: {1: (2, l), 2: (1, l), 3: (3, lon_n - 1 - l)}.get(b))
    swap_r = swap(lambda b, l: (b, l ^ 1))
    swap_s = swap(lambda b, l: (b, (((l + 1) ^ 1) - 1) % lon_n))

    q = tracers.reshape(NT * LEV * ROWS, COLS)
    ve = vel_east.reshape(LEV * ROWS, COLS)
    vn = vel_north.reshape(LEV * ROWS, COLS)
    lm = land_mask.reshape(LEV * ROWS, COLS)
    slot = float_slots(float_owner)
    out_p, out_q = pack_rows(tracers, vel_east, vel_north, land_mask, step_area)
    in_q = swap_q(out_q)
    in_p = swap_p(out_p)
    out_r, out_s = pack_cols(q, ve, vn, lm, step_area, in_p, in_q)
    in_s = swap_s(out_s)
    in_r = swap_r(out_r)
    out, outbox = both_steps(q, ve, vn, lm, step_area, in_p, in_q, in_r, in_s, float_cell, slot, lat_n * lon_n)
    inbox = lax.all_to_all(
        outbox.reshape(lat_n * lon_n, CAP, NT * LEV), axes, split_axis=0, concat_axis=0, tiled=True
    ).reshape(lat_n * lon_n * CAP, NT * LEV)
    arrivals, counts = unpack_arrivals(inbox)
    return out.reshape(tracers.shape), arrivals, counts.reshape(-1)


def solution(mesh):
    placed = (
        P(None, None, "lat", "lon"),
        P(None, "lat", "lon"),
        P(None, "lat", "lon"),
        P(None, "lat", "lon"),
        P("lat", "lon"),
        P(("lat", "lon")),
        P(("lat", "lon"), None),
    )
    return jax.shard_map(
        local,
        mesh=mesh,
        in_specs=placed,
        out_specs=(P(None, None, "lat", "lon"), P(("lat", "lon"), None), P(("lat", "lon"))),
        check_vma=False,
    )
```

```python
import jax
import jax.numpy as jnp
from jax import lax
from jax.experimental import pallas as pl
from jax.experimental.pallas import tpu as pltpu
from jax.sharding import PartitionSpec as P

CAP = 4
NT, LEV, ROWS, COLS = 4, 32, 32, 128
KG = LEV // 8
LANES = NT * LEV
SLOTS = 24
S_VE, S_VN, S_M = 16, 18, 21
ABSENT = 1e30
SIXTH = 1.0 / 6.0

WIDE, PAD = COLS + 16, 8
Q0 = 0
VE = Q0 + (ROWS + 8) * WIDE
VN = VE + (ROWS + 4) * WIDE
MS = VN + (ROWS + 6) * WIDE
Q1 = MS + (ROWS + 6) * WIDE
UE = Q1 + (ROWS + 4) * WIDE
UN = UE + (ROWS + 4) * WIDE
Q2 = UN + (ROWS + 6) * WIDE
CELLS = Q2 + ROWS * COLS
MSG = (ROWS + 4) * 4


def lanes():
    return lax.broadcasted_iota(jnp.int32, (8, COLS), 1)


def pick(x, index):
    return jnp.take_along_axis(x, index, axis=1, mode="promise_in_bounds")


def full(shape, dtype=jnp.float32):
    return jax.ShapeDtypeStruct(shape, dtype)


def params(mib):
    return pltpu.CompilerParams(vmem_limit_bytes=mib * 1024 * 1024)


def vmem():
    return pl.BlockSpec(memory_space=pltpu.VMEM)


def rows_kernel(q_lo, q_hi, ve_lo, ve_hi, vn_lo, vn_hi, lm_lo, lm_hi, area, out_p, out_q):
    lat = lax.axis_index("lat")
    even = lat % 2 == 0
    fold = lat == 3
    flip = COLS - 1 - lanes()

    def take(ref, plane, row):
        return ref[pl.ds(plane * 8 + row, 8, stride=8), :]

    def mass(ref, kg, row, at):
        wet = take(ref, kg * 8, row).astype(jnp.float32)
        return wet * jnp.broadcast_to(area[at : at + 1, :], (8, COLS))

    for kg in range(KG):

        def put(slot, bottom, normal, mirrored):
            top = jnp.where(fold, pick(mirrored, flip), normal)
            out_p[slot, kg * 8 : kg * 8 + 8, :] = jnp.where(even, top, bottom)
            out_q[slot, kg * 8 : kg * 8 + 8, :] = jnp.where(even, bottom, top)

        for c in range(NT):
            plane = c * LEV + kg * 8
            low = [take(q_lo, plane, r) for r in range(4)]
            high = [take(q_hi, plane, 4 + r) for r in range(4)]
            for r in range(4):
                put(c * 4 + r, low[r], high[r], high[3 - r])
        low = [take(ve_lo, kg * 8, r) for r in range(2)]
        high = [take(ve_hi, kg * 8, 6 + r) for r in range(2)]
        for r in range(2):
            put(S_VE + r, low[r], high[r], -high[1 - r])
        low = [take(vn_lo, kg * 8, r) for r in (0, 0, 1)]
        high = [take(vn_hi, kg * 8, 5 + r) for r in range(3)]
        for r in range(3):
            put(S_VN + r, low[r], high[r], -high[2 - r])
        low = [mass(lm_lo, kg, r, r) for r in range(3)]
        high = [mass(lm_hi, kg, 5 + r, 29 + r) for r in range(3)]
        for r in range(3):
            put(S_M + r, low[r], high[r], high[2 - r])


def pack_rows(tracers, ve, vn, lm, area):
    def spec(n, at):
        return pl.BlockSpec((n, 8, COLS), lambda i: (0, at, 0))

    def body(*refs):
        refs = list(refs)
        flat = [r.reshape(r.shape[0] * 8, COLS) for r in refs[:8]]
        rows_kernel(*flat, *refs[8:])

    q3 = tracers.reshape(NT * LEV, ROWS, COLS)
    return pl.pallas_call(
        body,
        grid=(1,),
        in_specs=[
            spec(NT * LEV, 0), spec(NT * LEV, 3), spec(LEV, 0), spec(LEV, 3),
            spec(LEV, 0), spec(LEV, 3), spec(LEV, 0), spec(LEV, 3),
            pl.BlockSpec((ROWS, COLS), lambda i: (0, 0)),
        ],
        out_specs=[pl.BlockSpec((SLOTS, LEV, COLS), lambda i: (0, 0, 0))] * 2,
        out_shape=[full((SLOTS, LEV, COLS))] * 2,
        compiler_params=params(12),
        name="pack_rows",
    )(q3, q3, ve, ve, vn, vn, lm, lm, area)


def at(section, row, col):
    return section + row * WIDE + PAD + col


def to_lanes(planes):
    return jnp.concatenate(planes, axis=0).T


def float_slots(owner, slot):
    n = owner.shape[1]
    mine = owner[...].astype(jnp.float32)
    rank = jnp.zeros((1, n), jnp.float32)
    for start in range(0, n, COLS):
        theirs = jnp.broadcast_to(mine[:, start : start + COLS], (COLS, COLS)).T
        earlier = lax.broadcasted_iota(jnp.int32, (COLS, n), 0) + start < lax.broadcasted_iota(jnp.int32, (COLS, n), 1)
        same = jnp.concatenate([theirs] * (n // COLS), axis=1) == jnp.broadcast_to(mine, (COLS, n))
        rank = rank + jnp.sum(jnp.where(same & earlier, 1.0, 0.0), axis=0, keepdims=True)
    slot[...] = owner[...] * CAP + rank.astype(jnp.int32)


def load_kernel(q, ve, vn, lm, area, owner, big, slot):
    float_slots(owner, slot)

    def step(row, _):
        def own(ref, plane):
            return ref[pl.ds(plane * ROWS + row, 8, stride=ROWS), :]

        def keep(section, row, planes):
            big[pl.ds(pl.multiple_of(at(section, row, 0), 8), COLS), :] = to_lanes(planes)

        keep(Q0, row + 4, [own(q, p * 8) for p in range(LANES // 8)])
        keep(VE, row + 2, [own(ve, kg * 8) * SIXTH for kg in range(KG)] * NT)
        keep(VN, row + 3, [own(vn, kg * 8) * SIXTH for kg in range(KG)] * NT)
        size = jnp.broadcast_to(area[pl.ds(row, 1), :], (8, COLS))
        keep(MS, row + 3, [own(lm, kg * 8).astype(jnp.float32) * size for kg in range(KG)] * NT)
        return 0

    lax.fori_loop(0, ROWS, step, 0)


def load_cells(q, ve, vn, lm, area, owner):
    return pl.pallas_call(
        load_kernel,
        in_specs=[vmem()] * 6,
        out_specs=[vmem()] * 2,
        out_shape=[full((CELLS, LANES)), full(owner.shape, jnp.int32)],
        compiler_params=params(8),
        cost_estimate=pl.CostEstimate(flops=0, bytes_accessed=16_000_000, transcendentals=0),
        name="load_cells",
    )(q, ve, vn, lm, area, owner)


def ghost_kernel(big_in, in_p, in_q, big, out_r, out_s):
    lat_even = lax.axis_index("lat") % 2 == 0
    fold = lax.axis_index("lat") == 3
    shift = jnp.where(fold, 1, 0)
    lon_even = lax.axis_index("lon") % 2 == 0
    to_r = jnp.where(lon_even, COLS - 4, 0)
    to_s = COLS - 4 - to_r

    def ghost(north, slot):
        a, b = (in_p, in_q) if north else (in_q, in_p)
        return [
            jnp.where(lat_even, a[slot, kg * 8 : kg * 8 + 8, :], b[slot, kg * 8 : kg * 8 + 8, :]) for kg in range(KG)
        ]

    def keep(section, row, planes, back=0):
        big[pl.ds(at(section, row, 0) - back, COLS), :] = to_lanes(planes)

    def static(north, slot, scale):
        return [x * scale for x in ghost(north, slot)] * NT

    for north in (False, True):
        for r in range(4):
            planes = [x for c in range(NT) for x in ghost(north, c * 4 + r)]
            keep(Q0, ROWS + 4 + r if north else r, planes)
        for r in range(2):
            keep(VE, ROWS + 2 + r if north else r, static(north, S_VE + r, SIXTH), shift if north else 0)
        for r in range(3):
            if north and r == 0:
                theirs = to_lanes(static(north, S_VN, SIXTH))
                ours = big[pl.ds(at(VN, ROWS + 2, 0), COLS), :]
                big[pl.ds(at(VN, ROWS + 5, 0), COLS), :] = jnp.where(fold, theirs, ours)
            else:
                keep(VN, ROWS + 2 + r if north else r, static(north, S_VN + r, SIXTH))
            keep(MS, ROWS + 3 + r if north else r, static(north, S_M + r, 1.0))

    group = lax.broadcasted_iota(jnp.int32, (4, LANES), 1) // LEV

    def send(row, back):
        for out, col in ((out_r, to_r), (out_s, to_s)):
            out[pl.ds(row * 4, 4), :] = big[pl.ds(at(Q0, row + 2, 0) + col, 4), :]
            east = big[pl.ds(at(VE, row, 0) + col - back, 4), :]
            north = big[pl.ds(at(VN, row + 1, 0) + col, 4), :]
            mass = big[pl.ds(at(MS, row + 1, 0) + col, 4), :]
            mixed = jnp.where(group == 0, east, jnp.where(group == 1, north, mass))
            out[pl.ds(MSG + row * 4, 4), :] = mixed

    def some(i, _):
        for j in range(4):
            send(2 + i * 4 + j, 0)
        return 0

    for row in (0, 1):
        send(row, 0)
    lax.fori_loop(0, ROWS // 4, some, 0)
    for row in (ROWS + 2, ROWS + 3):
        send(row, shift)


def ghost_rows(big, in_p, in_q):
    return pl.pallas_call(
        ghost_kernel,
        in_specs=[vmem()] * 3,
        out_specs=[vmem()] * 3,
        out_shape=[full((CELLS, LANES)), full((2 * MSG, LANES)), full((2 * MSG, LANES))],
        input_output_aliases={0: 0},
        compiler_params=params(8),
        name="ghost_rows",
    )(big, in_p, in_q)


def advance(big, flux, step, x_blocks, y_blocks):
    first = step == 0
    low, high = (-2, ROWS + 2) if first else (0, ROWS)
    src, src_row = (Q0, 4) if first else (Q1, 2)

    def x_row(r, _):
        def cells(section, row, col):
            return big[pl.ds(at(section, row + low, col) + r * WIDE, 8), :]

        for block in x_blocks:
            col = block * 8
            cur = cells(src, src_row, col)
            left = cells(src, src_row, col - 1)
            right = cells(src, src_row, col + 1)
            far = cells(src, src_row, col + 2)
            if first:
                w = cells(VE, 2, col)
                mass = jnp.minimum(cells(MS, 3, col), cells(MS, 3, col + 1))
                w = jnp.where(mass > 0, w, 0.0)
                big[pl.ds(at(UE, 2 + low, col) + r * WIDE, 8), :] = w
            else:
                w = cells(UE, 2, col)
            both = cur + right
            side = jnp.where(w > 0, 3.0 * cur - left, 3.0 * right - far)
            flux[pl.ds(at(PAD, 2 + low, col) + r * WIDE, 8), :] = w * (both + both + side)
        return 0

    lax.fori_loop(0, high - low, x_row, 0)

    def y_block(start, b):
        ahead = pl.multiple_of(b * 8, 8)

        def cells(section, row):
            return pl.ds(at(section, row, start * 8) + ahead, 8)

        def face(row, e, index=None):
            index = row + 3 if index is None else index
            if first:
                w = big[cells(VN, index), :]
                mass = jnp.minimum(big[cells(MS, row + 3), :], big[cells(MS, row + 4), :])
                w = jnp.where(mass > 0, w, 0.0)
                big[cells(UN, index), :] = w
            else:
                w = big[cells(UN, index), :]
            both = e[row] + e[row + 1]
            side = jnp.where(w > 0, 3.0 * e[row] - e[row - 1], 3.0 * e[row + 1] - e[row + 2])
            return w * (both + both + side)

        e = {row: big[cells(src, row + src_row), :] for row in range(low - 2, low + 2)}
        below = face(low - 1, e)
        for row in range(low, high):
            e[row + 2] = big[cells(src, row + src_row + 2), :]
            if row == ROWS:
                below = face(ROWS - 1, e, ROWS + 5)
            above = face(row, e)
            across = flux[cells(PAD, row + 2), :] - flux[cells(PAD - 1, row + 2), :]
            new = e[row] - big[cells(MS, row + 3), :] * (across + (above - below))
            if first:
                big[cells(Q1, row + 2), :] = new
            else:
                big[pl.ds(Q2 + row * COLS + start * 8 + ahead, 8), :] = new
            below = above

    for start, stop in y_blocks:

        def one(b, _, start=start):
            y_block(start, b)
            return 0

        lax.fori_loop(0, stop - start, one, 0)


def inner_kernel(big_in, big, flux):
    advance(big, flux, 0, range(0, 15), [(1, 15)])
    advance(big, flux, 1, range(1, 14), [(2, 14)])


def inner_steps(big):
    return pl.pallas_call(
        inner_kernel,
        in_specs=[vmem()],
        out_specs=vmem(),
        out_shape=full((CELLS, LANES)),
        scratch_shapes=[pltpu.VMEM(((ROWS + 4) * WIDE + PAD, LANES), jnp.float32)],
        input_output_aliases={0: 0},
        compiler_params=params(8),
        cost_estimate=pl.CostEstimate(flops=40_000_000, bytes_accessed=20_000_000, transcendentals=0),
        name="inner_steps",
    )(big)


def outer_kernel(big_in, in_r, in_s, cell, slot, big, outbox, after, flux, done):
    even = lax.axis_index("lon") % 2 == 0
    shift = jnp.where(lax.axis_index("lat") == 3, 1, 0)
    lane = lax.broadcasted_iota(jnp.int32, (8, LANES), 1)

    def receive(pair, back):
        rows = pl.ds(pl.multiple_of(pair * 8, 8), 8)
        more = pl.ds(pl.multiple_of(MSG + pair * 8, 8), 8)
        for west, col in ((True, -4), (False, COLS)):
            a, b = (in_s, in_r) if west else (in_r, in_s)
            q = jnp.where(even, a[rows, :], b[rows, :])
            mixed = jnp.where(even, a[more, :], b[more, :])
            parts = [pick(mixed, g * LEV + lane % LEV) for g in range(3)]
            for half in range(2):
                row = pair * 2 + half
                h = slice(half * 4, half * 4 + 4)
                big[pl.ds(at(Q0, row + 2, col), 4), :] = q[h]
                big[pl.ds(at(VE, row, col) - back, 4), :] = parts[0][h]
                big[pl.ds(at(VN, row + 1, col), 4), :] = parts[1][h]
                big[pl.ds(at(MS, row + 1, col), 4), :] = parts[2][h]

    def inside(i, _):
        for j in range(2):
            receive(1 + i * 2 + j, 0)
        return 0

    receive(0, 0)
    lax.fori_loop(0, ROWS // 4, inside, 0)
    receive(ROWS // 2 + 1, shift)

    advance(big, flux, 0, (-1, 0, 14, 15, 16), [(-1, 1), (15, 17)])
    advance(big, flux, 1, (-1, 0, 1, 13, 14, 15), [(0, 2), (14, 16)])

    keep = pltpu.make_async_copy(big.at[pl.ds(Q2, ROWS * COLS), :], after, done)
    keep.start()

    mark = jnp.where(lane == 0, ABSENT, 0.0)
    for i in range(outbox.shape[0] // 8):
        outbox[i * 8 : i * 8 + 8, :] = mark

    def send(i, _):
        for j in range(8):
            outbox[pl.ds(slot[i * 8 + j], 1), :] = big[pl.ds(Q2 + cell[i * 8 + j], 1), :]
        return 0

    lax.fori_loop(0, cell.shape[0] // 8, send, 0)
    keep.wait()


def outer_steps(big, in_r, in_s, cell, slot, devices):
    smem = pl.BlockSpec(memory_space=pltpu.SMEM)
    return pl.pallas_call(
        outer_kernel,
        in_specs=[vmem()] * 3 + [smem, smem],
        out_specs=[vmem(), vmem(), pl.BlockSpec(memory_space=pl.ANY)],
        out_shape=[full((CELLS, LANES)), full((devices * CAP, LANES)), full((ROWS * COLS, LANES))],
        scratch_shapes=[pltpu.VMEM(((ROWS + 4) * WIDE + PAD, LANES), jnp.float32), pltpu.SemaphoreType.DMA(())],
        input_output_aliases={0: 0},
        compiler_params=params(8),
        name="outer_steps",
    )(big, in_r, in_s, cell, slot)


def store_kernel(after, out):
    def step(row, _):
        x = after[pl.ds(pl.multiple_of(row * COLS, 8), COLS), :].T
        for p in range(LANES // 8):
            out[pl.ds(p * 8 * ROWS + row, 8, stride=ROWS), :] = x[p * 8 : p * 8 + 8]
        return 0

    lax.fori_loop(0, ROWS, step, 0)


def store_cells(after):
    return pl.pallas_call(
        store_kernel,
        in_specs=[vmem()],
        out_specs=vmem(),
        out_shape=full((LANES * ROWS, COLS)),
        compiler_params=params(4),
        cost_estimate=pl.CostEstimate(flops=0, bytes_accessed=8_000_000, transcendentals=0),
        name="store_cells",
    )(after)


def arrivals_kernel(inbox, out, counts):
    total = jnp.zeros((8, COLS), jnp.float32)
    sub = lax.broadcasted_iota(jnp.int32, (8, COLS), 0)
    lane = lanes()
    for i in range(inbox.shape[0] // 8):
        x = inbox[i * 8 : i * 8 + 8, :]
        here = jnp.broadcast_to(x[:, 0:1], (8, COLS)) < ABSENT * 0.5
        out[i * 8 : i * 8 + 8, :] = jnp.where(here, x, 0.0)
        total = total + jnp.where(here & (lane == (i * 8 + sub) // CAP), 1.0, 0.0)
    counts[...] = jnp.sum(total, axis=0, keepdims=True).astype(jnp.int32)


def unpack_arrivals(inbox):
    n = inbox.shape[0]
    return pl.pallas_call(
        arrivals_kernel,
        out_shape=[full(inbox.shape), full((1, n // CAP), jnp.int32)],
        compiler_params=params(4),
        name="unpack_arrivals",
    )(inbox)


def local(tracers, vel_east, vel_north, land_mask, step_area, float_cell, float_owner):
    lat_n, lon_n = lax.axis_size("lat"), lax.axis_size("lon")
    axes = ("lat", "lon")

    def swap(target):
        pairs = []
        for b in range(lat_n):
            for l in range(lon_n):
                to = target(b, l)
                if to is not None:
                    pairs.append((b * lon_n + l, to[0] * lon_n + to[1]))
        return lambda x: lax.ppermute(x, axes, pairs)

    swap_p = swap(lambda b, l: (b ^ 1, l))
    swap_q = swap(lambda b, l: {1: (2, l), 2: (1, l), 3: (3, lon_n - 1 - l)}.get(b))
    swap_r = swap(lambda b, l: (b, l ^ 1))
    swap_s = swap(lambda b, l: (b, (((l + 1) ^ 1) - 1) % lon_n))

    q = tracers.reshape(NT * LEV * ROWS, COLS)
    ve = vel_east.reshape(LEV * ROWS, COLS)
    vn = vel_north.reshape(LEV * ROWS, COLS)
    lm = land_mask.reshape(LEV * ROWS, COLS)
    out_p, out_q = pack_rows(tracers, vel_east, vel_north, land_mask, step_area)
    in_q = swap_q(out_q)
    in_p = swap_p(out_p)
    big, slot = load_cells(q, ve, vn, lm, step_area, float_owner.reshape(1, -1))
    big, out_r, out_s = ghost_rows(big, in_p, in_q)
    in_s = swap_s(out_s)
    in_r = swap_r(out_r)
    big = inner_steps(big)
    _, outbox, after = outer_steps(big, in_r, in_s, float_cell, slot.reshape(-1), lat_n * lon_n)
    inbox = lax.all_to_all(
        outbox.reshape(lat_n * lon_n, CAP, NT * LEV), axes, split_axis=0, concat_axis=0, tiled=True
    ).reshape(lat_n * lon_n * CAP, NT * LEV)
    out = store_cells(after)
    arrivals, counts = unpack_arrivals(inbox)
    return out.reshape(tracers.shape), arrivals, counts.reshape(-1)


def solution(mesh):
    placed = (
        P(None, None, "lat", "lon"),
        P(None, "lat", "lon"),
        P(None, "lat", "lon"),
        P(None, "lat", "lon"),
        P("lat", "lon"),
        P(("lat", "lon")),
        P(("lat", "lon"), None),
    )
    return jax.shard_map(
        local,
        mesh=mesh,
        in_specs=placed,
        out_specs=(P(None, None, "lat", "lon"), P(("lat", "lon"), None), P(("lat", "lon"))),
        check_vma=False,
    )
```

```python
import jax
import jax.numpy as jnp
from jax import lax
from jax.experimental import pallas as pl
from jax.experimental.pallas import tpu as pltpu
from jax.sharding import PartitionSpec as P

CAP = 4
NT, LEV, ROWS, COLS = 4, 32, 32, 128
KG = LEV // 8
LANES = NT * LEV
SLOTS = 24
S_VE, S_VN, S_M = 16, 18, 21
ABSENT = 1e30
SIXTH = 1.0 / 6.0

WIDE, PAD = COLS + 16, 8
Q0 = 0
VE = Q0 + (ROWS + 8) * WIDE
VN = VE + (ROWS + 4) * WIDE
MS = VN + (ROWS + 6) * WIDE
Q1 = MS + (ROWS + 6) * WIDE
UE = Q1 + (ROWS + 4) * WIDE
UN = UE + (ROWS + 4) * WIDE
CELLS = UN + (ROWS + 6) * WIDE
MSG = (ROWS + 4) * 4


def lanes():
    return lax.broadcasted_iota(jnp.int32, (8, COLS), 1)


def pick(x, index):
    return jnp.take_along_axis(x, index, axis=1, mode="promise_in_bounds")


def full(shape, dtype=jnp.float32):
    return jax.ShapeDtypeStruct(shape, dtype)


def params(mib):
    return pltpu.CompilerParams(vmem_limit_bytes=int(mib * 1024 * 1024))


def vmem():
    return pl.BlockSpec(memory_space=pltpu.VMEM)


def rows_kernel(q, ve, vn, lm, area, out_p, out_q):
    lat = lax.axis_index("lat")
    even = lat % 2 == 0
    fold = lat == 3
    flip = COLS - 1 - lanes()

    def take(pair, plane, row):
        return pair[row // 16][pl.ds(plane * 8 + row % 8, 8, stride=8), :]

    def mass(kg, row):
        wet = take(lm, kg * 8, row).astype(jnp.float32)
        return wet * jnp.broadcast_to(area[row : row + 1, :], (8, COLS))

    top = ROWS - 4
    for kg in range(KG):

        def put(slot, bottom, normal, mirrored):
            upper = jnp.where(fold, pick(mirrored, flip), normal)
            out_p[slot, kg * 8 : kg * 8 + 8, :] = jnp.where(even, upper, bottom)
            out_q[slot, kg * 8 : kg * 8 + 8, :] = jnp.where(even, bottom, upper)

        for c in range(NT):
            plane = c * LEV + kg * 8
            low = [take(q, plane, r) for r in range(4)]
            high = [take(q, plane, top + r) for r in range(4)]
            for r in range(4):
                put(c * 4 + r, low[r], high[r], high[3 - r])
        low = [take(ve, kg * 8, r) for r in range(2)]
        high = [take(ve, kg * 8, top + 2 + r) for r in range(2)]
        for r in range(2):
            put(S_VE + r, low[r], high[r], -high[1 - r])
        low = [take(vn, kg * 8, r) for r in (0, 0, 1)]
        high = [take(vn, kg * 8, top + 1 + r) for r in range(3)]
        for r in range(3):
            put(S_VN + r, low[r], high[r], -high[2 - r])
        low = [mass(kg, r) for r in range(3)]
        high = [mass(kg, top + 1 + r) for r in range(3)]
        for r in range(3):
            put(S_M + r, low[r], high[r], high[2 - r])


def pack_rows(q, ve, vn, lm, area):
    def body(*refs):
        tiles = [r.reshape(r.shape[0] * 8, COLS) for r in refs[:8]]
        rows_kernel(*[tiles[2 * k : 2 * k + 2] for k in range(4)], *refs[8:])

    def tile(n, at_tile):
        return pl.BlockSpec((n, 8, COLS), lambda i: (0, at_tile, 0))

    def whole(shape):
        return pl.BlockSpec(shape, lambda i: (0,) * len(shape))

    last = ROWS // 8 - 1
    outs = [full((SLOTS, LEV, COLS))] * 2
    return pl.pallas_call(
        body,
        grid=(1,),
        in_specs=[tile(x.shape[0], t) for x in (q, ve, vn, lm) for t in (0, last)] + [whole(area.shape)],
        out_specs=[whole(x.shape) for x in outs],
        out_shape=outs,
        compiler_params=params(53),
        name="pack_rows",
    )(q, q, ve, ve, vn, vn, lm, lm, area)


def pass_on(*messages):
    anywhere = [pl.BlockSpec(memory_space=pl.ANY)] * len(messages)
    return pl.pallas_call(
        lambda *refs: None,
        in_specs=anywhere,
        out_specs=anywhere,
        out_shape=[full(m.shape) for m in messages],
        input_output_aliases={k: k for k in range(len(messages))},
        compiler_params=pltpu.CompilerParams(vmem_limit_bytes=1024 * 1024, has_side_effects=True),
        cost_estimate=pl.CostEstimate(flops=30_000_000_000, bytes_accessed=0, transcendentals=0),
        name="pass_on",
    )(*messages)


def at(section, row, col):
    return section + row * WIDE + PAD + col


def to_lanes(planes):
    return jnp.concatenate(planes, axis=0).T


def load_kernel(q, ve, vn, lm, area, big):
    def one(row):
        def own(ref, plane):
            return ref[pl.ds(plane * ROWS + row, 8, stride=ROWS), :]

        def keep(section, row, planes):
            big[pl.ds(pl.multiple_of(at(section, row, 0), 8), COLS), :] = to_lanes(planes)

        keep(Q0, row + 4, [own(q, p * 8) for p in range(LANES // 8)])
        keep(VE, row + 2, [own(ve, kg * 8) * SIXTH for kg in range(KG)] * NT)
        keep(VN, row + 3, [own(vn, kg * 8) * SIXTH for kg in range(KG)] * NT)
        size = jnp.broadcast_to(area[pl.ds(row, 1), :], (8, COLS))
        keep(MS, row + 3, [own(lm, kg * 8).astype(jnp.float32) * size for kg in range(KG)] * NT)

    def four(i, _):
        for j in range(4):
            one(i * 4 + j)
        return 0

    lax.fori_loop(0, ROWS // 4, four, 0)


def load_cells(q, ve, vn, lm, area):
    q, ve, vn, lm = [x.reshape(-1, COLS) for x in (q, ve, vn, lm)]
    return pl.pallas_call(
        load_kernel,
        in_specs=[vmem()] * 5,
        out_specs=vmem(),
        out_shape=full((CELLS, LANES)),
        compiler_params=params(8),
        cost_estimate=pl.CostEstimate(flops=0, bytes_accessed=16_000_000, transcendentals=0),
        name="load_cells",
    )(q, ve, vn, lm, area)


def ghost_kernel(big_in, in_p, in_q, big, out_r, out_s):
    lat_even = lax.axis_index("lat") % 2 == 0
    fold = lax.axis_index("lat") == 3
    shift = jnp.where(fold, 1, 0)
    lon_even = lax.axis_index("lon") % 2 == 0
    to_r = jnp.where(lon_even, COLS - 4, 0)
    to_s = COLS - 4 - to_r

    def ghost(north, slot):
        a, b = (in_p, in_q) if north else (in_q, in_p)
        return [
            jnp.where(lat_even, a[slot, kg * 8 : kg * 8 + 8, :], b[slot, kg * 8 : kg * 8 + 8, :]) for kg in range(KG)
        ]

    def keep(section, row, planes, back=0):
        big[pl.ds(at(section, row, 0) - back, COLS), :] = to_lanes(planes)

    def static(north, slot, scale):
        return [x * scale for x in ghost(north, slot)] * NT

    for north in (False, True):
        for r in range(4):
            planes = [x for c in range(NT) for x in ghost(north, c * 4 + r)]
            keep(Q0, ROWS + 4 + r if north else r, planes)
        for r in range(2):
            keep(VE, ROWS + 2 + r if north else r, static(north, S_VE + r, SIXTH), shift if north else 0)
        for r in range(3):
            if north and r == 0:
                theirs = to_lanes(static(north, S_VN, SIXTH))
                ours = big[pl.ds(at(VN, ROWS + 2, 0), COLS), :]
                big[pl.ds(at(VN, ROWS + 5, 0), COLS), :] = jnp.where(fold, theirs, ours)
            else:
                keep(VN, ROWS + 2 + r if north else r, static(north, S_VN + r, SIXTH))
            keep(MS, ROWS + 3 + r if north else r, static(north, S_M + r, 1.0))

    group = lax.broadcasted_iota(jnp.int32, (4, LANES), 1) // LEV

    def send(row, back):
        for out, col in ((out_r, to_r), (out_s, to_s)):
            out[pl.ds(row * 4, 4), :] = big[pl.ds(at(Q0, row + 2, 0) + col, 4), :]
            east = big[pl.ds(at(VE, row, 0) + col - back, 4), :]
            north = big[pl.ds(at(VN, row + 1, 0) + col, 4), :]
            mass = big[pl.ds(at(MS, row + 1, 0) + col, 4), :]
            mixed = jnp.where(group == 0, east, jnp.where(group == 1, north, mass))
            out[pl.ds(MSG + row * 4, 4), :] = mixed

    def some(i, _):
        for j in range(4):
            send(2 + i * 4 + j, 0)
        return 0

    for row in (0, 1):
        send(row, 0)
    lax.fori_loop(0, ROWS // 4, some, 0)
    for row in (ROWS + 2, ROWS + 3):
        send(row, shift)


def ghost_rows(big, in_p, in_q):
    return pl.pallas_call(
        ghost_kernel,
        in_specs=[vmem()] * 3,
        out_specs=[vmem()] * 3,
        out_shape=[full((CELLS, LANES)), full((2 * MSG, LANES)), full((2 * MSG, LANES))],
        input_output_aliases={0: 0},
        compiler_params=params(8),
        name="ghost_rows",
    )(big, in_p, in_q)


def advance(big, after, flux, step, runs, x_blocks, y_blocks):
    for low, high in runs:
        across_columns(big, flux, step, low, high, x_blocks)
    for start, stop in y_blocks:

        def one(b, _, start=start):
            for low, high in runs:
                across_rows(big, after, flux, step, low, high, start, b)
            return 0

        lax.fori_loop(0, stop - start, one, 0)


def across_columns(big, flux, step, low, high, x_blocks):
    first = step == 0
    src, src_row = (Q0, 4) if first else (Q1, 2)

    def x_row(r):
        def cells(section, row, col):
            return big[pl.ds(at(section, row + low, col) + r * WIDE, 8), :]

        for block in x_blocks:
            col = block * 8
            cur = cells(src, src_row, col)
            left = cells(src, src_row, col - 1)
            right = cells(src, src_row, col + 1)
            far = cells(src, src_row, col + 2)
            if first:
                w = cells(VE, 2, col)
                mass = jnp.minimum(cells(MS, 3, col), cells(MS, 3, col + 1))
                w = jnp.where(mass > 0, w, 0.0)
                opened.append((at(UE, 2 + low, col) + r * WIDE, w))
            else:
                w = cells(UE, 2, col)
            both = cur + right
            side = jnp.where(w > 0, 3.0 * cur - left, 3.0 * right - far)
            fluxes.append((at(PAD, 2 + low, col) + r * WIDE, w * (both + both + side)))

    def x_rows(i, _):
        fluxes.clear()
        opened.clear()
        for j in range(unroll):
            x_row(i * unroll + j)
        for start, w in opened:
            big[pl.ds(start, 8), :] = w
        for start, f in fluxes:
            flux[pl.ds(start, 8), :] = f
        return 0

    fluxes, opened = [], []
    unroll = 4 if len(x_blocks) < 8 else 1
    lax.fori_loop(0, (high - low) // unroll, x_rows, 0)


def across_rows(big, after, flux, step, low, high, start, b):
    first = step == 0
    src, src_row = (Q0, 4) if first else (Q1, 2)
    ahead = pl.multiple_of(b * 8, 8)

    def cells(section, row):
        return pl.ds(at(section, row, start * 8) + ahead, 8)

    def face(row, e, index=None):
        index = row + 3 if index is None else index
        if first:
            w = big[cells(VN, index), :]
            mass = jnp.minimum(big[cells(MS, row + 3), :], big[cells(MS, row + 4), :])
            w = jnp.where(mass > 0, w, 0.0)
            big[cells(UN, index), :] = w
        else:
            w = big[cells(UN, index), :]
        both = e[row] + e[row + 1]
        side = jnp.where(w > 0, 3.0 * e[row] - e[row - 1], 3.0 * e[row + 1] - e[row + 2])
        return w * (both + both + side)

    e = {row: big[cells(src, row + src_row), :] for row in range(low - 2, low + 2)}
    below = face(low - 1, e)
    for row in range(low, high):
        e[row + 2] = big[cells(src, row + src_row + 2), :]
        if row == ROWS:
            below = face(ROWS - 1, e, ROWS + 5)
        above = face(row, e)
        across = flux[cells(PAD, row + 2), :] - flux[cells(PAD - 1, row + 2), :]
        new = e[row] - big[cells(MS, row + 3), :] * (across + (above - below))
        if first:
            big[cells(Q1, row + 2), :] = new
        else:
            after[pl.ds(row * COLS + start * 8 + ahead, 8), :] = new
        below = above


ALL = ((-2, ROWS + 2),), ((0, ROWS),)


def flux_scratch():
    return pltpu.VMEM(((ROWS + 4) * WIDE + PAD, LANES), jnp.float32)


def float_slots(owner, slot):
    n = owner.shape[1]
    mine = owner[...].astype(jnp.float32)
    rank = jnp.zeros((1, n), jnp.float32)
    for start in range(0, n, COLS):
        theirs = jnp.broadcast_to(mine[:, start : start + COLS], (COLS, COLS)).T
        earlier = lax.broadcasted_iota(jnp.int32, (COLS, n), 0) + start < lax.broadcasted_iota(jnp.int32, (COLS, n), 1)
        same = jnp.concatenate([theirs] * (n // COLS), axis=1) == jnp.broadcast_to(mine, (COLS, n))
        rank = rank + jnp.sum(jnp.where(same & earlier, 1.0, 0.0), axis=0, keepdims=True)
    slot[...] = owner[...] * CAP + rank.astype(jnp.int32)


def inner_kernel(big_in, owner, big, after, slot, flux):
    float_slots(owner, slot)
    advance(big, after, flux, 0, ALL[0], range(0, 15), [(1, 15)])
    advance(big, after, flux, 1, ALL[1], range(1, 14), [(2, 14)])


def inner_steps(big, owner):
    return pl.pallas_call(
        inner_kernel,
        in_specs=[vmem()] * 2,
        out_specs=[vmem()] * 3,
        out_shape=[full((CELLS, LANES)), full((ROWS * COLS, LANES)), full(owner.shape, jnp.int32)],
        scratch_shapes=[flux_scratch()],
        input_output_aliases={0: 0},
        compiler_params=params(6),
        cost_estimate=pl.CostEstimate(flops=40_000_000, bytes_accessed=20_000_000, transcendentals=0),
        name="inner_steps",
    )(big, owner)


def outer_kernel(big_in, after_in, in_r, in_s, cell, slot, big, after, outbox, flux):
    even = lax.axis_index("lon") % 2 == 0
    shift = jnp.where(lax.axis_index("lat") == 3, 1, 0)
    lane = lax.broadcasted_iota(jnp.int32, (8, LANES), 1)

    def receive(pair, back):
        rows = pl.ds(pl.multiple_of(pair * 8, 8), 8)
        more = pl.ds(pl.multiple_of(MSG + pair * 8, 8), 8)
        for west, col in ((True, -4), (False, COLS)):
            a, b = (in_s, in_r) if west else (in_r, in_s)
            q = jnp.where(even, a[rows, :], b[rows, :])
            mixed = jnp.where(even, a[more, :], b[more, :])
            parts = [pick(mixed, g * LEV + lane % LEV) for g in range(3)]
            for half in range(2):
                row = pair * 2 + half
                h = slice(half * 4, half * 4 + 4)
                big[pl.ds(at(Q0, row + 2, col), 4), :] = q[h]
                big[pl.ds(at(VE, row, col) - back, 4), :] = parts[0][h]
                big[pl.ds(at(VN, row + 1, col), 4), :] = parts[1][h]
                big[pl.ds(at(MS, row + 1, col), 4), :] = parts[2][h]

    def inside(i, _):
        for j in range(2):
            receive(1 + i * 2 + j, 0)
        return 0

    receive(0, 0)
    lax.fori_loop(0, ROWS // 4, inside, 0)
    receive(ROWS // 2 + 1, shift)

    advance(big, after, flux, 0, ALL[0], (-1, 0, 14, 15, 16), [(-1, 1), (15, 17)])
    advance(big, after, flux, 1, ALL[1], (-1, 0, 1, 13, 14, 15), [(0, 2), (14, 16)])

    mark = jnp.where(lane == 0, ABSENT, 0.0)
    for i in range(outbox.shape[0] // 8):
        outbox[i * 8 : i * 8 + 8, :] = mark

    def send(i, _):
        to = [slot[i * 32 + j] for j in range(32)]
        rows = [after[pl.ds(cell[i * 32 + j], 1), :] for j in range(32)]
        for j in range(32):
            outbox[pl.ds(to[j], 1), :] = rows[j]
        return 0

    lax.fori_loop(0, cell.shape[0] // 32, send, 0)


def outer_steps(big, after, in_r, in_s, cell, slot, devices):
    smem = pl.BlockSpec(memory_space=pltpu.SMEM)
    return pl.pallas_call(
        outer_kernel,
        in_specs=[vmem()] * 4 + [smem, smem],
        out_specs=[vmem()] * 3,
        out_shape=[full((CELLS, LANES)), full((ROWS * COLS, LANES)), full((devices * CAP, LANES))],
        scratch_shapes=[flux_scratch()],
        input_output_aliases={0: 0, 1: 1},
        compiler_params=params(6),
        name="outer_steps",
    )(big, after, in_r, in_s, cell, slot)


def store_kernel(after, out):
    def step(row, _):
        x = after[pl.ds(pl.multiple_of(row * COLS, 8), COLS), :].T
        for p in range(LANES // 8):
            out[pl.ds(p * 8 * ROWS + row, 8, stride=ROWS), :] = x[p * 8 : p * 8 + 8]
        return 0

    lax.fori_loop(0, ROWS, step, 0)


def store_cells(after):
    return pl.pallas_call(
        store_kernel,
        in_specs=[vmem()],
        out_specs=vmem(),
        out_shape=full((LANES * ROWS, COLS)),
        compiler_params=params(4),
        cost_estimate=pl.CostEstimate(flops=0, bytes_accessed=8_000_000, transcendentals=0),
        name="store_cells",
    )(after)


def arrivals_kernel(inbox, out, counts):
    total = jnp.zeros((8, COLS), jnp.float32)
    sub = lax.broadcasted_iota(jnp.int32, (8, COLS), 0)
    lane = lanes()
    for i in range(inbox.shape[0] // 8):
        x = inbox[i * 8 : i * 8 + 8, :]
        here = jnp.broadcast_to(x[:, 0:1], (8, COLS)) < ABSENT * 0.5
        out[i * 8 : i * 8 + 8, :] = jnp.where(here, x, 0.0)
        total = total + jnp.where(here & (lane == (i * 8 + sub) // CAP), 1.0, 0.0)
    counts[...] = jnp.sum(total, axis=0, keepdims=True).astype(jnp.int32)


def unpack_arrivals(inbox):
    n = inbox.shape[0]
    return pl.pallas_call(
        arrivals_kernel,
        out_shape=[full(inbox.shape), full((1, n // CAP), jnp.int32)],
        compiler_params=params(4),
        name="unpack_arrivals",
    )(inbox)


def local(tracers, vel_east, vel_north, land_mask, step_area, float_cell, float_owner):
    lat_n, lon_n = lax.axis_size("lat"), lax.axis_size("lon")
    axes = ("lat", "lon")

    def swap(target):
        pairs = []
        for b in range(lat_n):
            for l in range(lon_n):
                to = target(b, l)
                if to is not None:
                    pairs.append((b * lon_n + l, to[0] * lon_n + to[1]))
        return lambda x: lax.ppermute(x, axes, pairs)

    swap_p = swap(lambda b, l: (b ^ 1, l))
    swap_q = swap(lambda b, l: {1: (2, l), 2: (1, l), 3: (3, lon_n - 1 - l)}.get(b))
    swap_r = swap(lambda b, l: (b, l ^ 1))
    swap_s = swap(lambda b, l: (b, (((l + 1) ^ 1) - 1) % lon_n))

    q = tracers.reshape(LANES, ROWS, COLS)
    fields = (q, vel_east, vel_north, land_mask, step_area)
    out_p, out_q = pack_rows(*fields)
    out_p, out_q = pass_on(out_p, out_q)
    in_q = swap_q(out_q)
    in_p = swap_p(out_p)
    big = load_cells(*fields)
    big, out_r, out_s = ghost_rows(big, in_p, in_q)
    in_s = swap_s(out_s)
    in_r = swap_r(out_r)
    big, after, slot = inner_steps(big, float_owner.reshape(1, -1))
    _, after, outbox = outer_steps(big, after, in_r, in_s, float_cell, slot.reshape(-1), lat_n * lon_n)
    inbox = lax.all_to_all(
        outbox.reshape(lat_n * lon_n, CAP, NT * LEV), axes, split_axis=0, concat_axis=0, tiled=True
    ).reshape(lat_n * lon_n * CAP, NT * LEV)
    out = store_cells(after)
    arrivals, counts = unpack_arrivals(inbox)
    return out.reshape(tracers.shape), arrivals, counts.reshape(-1)


def solution(mesh):
    placed = (
        P(None, None, "lat", "lon"),
        P(None, "lat", "lon"),
        P(None, "lat", "lon"),
        P(None, "lat", "lon"),
        P("lat", "lon"),
        P(("lat", "lon")),
        P(("lat", "lon"), None),
    )
    return jax.shard_map(
        local,
        mesh=mesh,
        in_specs=placed,
        out_specs=(P(None, None, "lat", "lon"), P(("lat", "lon"), None), P(("lat", "lon"))),
        check_vma=False,
    )
```

```python
import jax
import jax.numpy as jnp
from jax import lax
from jax.experimental import pallas as pl
from jax.experimental.pallas import tpu as pltpu
from jax.sharding import PartitionSpec as P


CAP = 4
NT, LEV, ROWS, COLS = 4, 32, 32, 128
KG = LEV // 8
LANES = NT * LEV
SLOTS = 23
S_VE, S_VN, S_M = 16, 18, 21
ABSENT = 1e30
SIXTH = 1.0 / 6.0

WIDE, PAD = COLS + 16, 8
Q0 = 0
VE = Q0 + (ROWS + 8) * WIDE
VN = VE + (ROWS + 4) * WIDE
MS = VN + (ROWS + 6) * WIDE
Q1 = MS + (ROWS + 6) * WIDE
UE = Q1 + (ROWS + 4) * WIDE
UN = UE + (ROWS + 4) * WIDE
CELLS = UN + (ROWS + 6) * WIDE
MSG = (ROWS + 4) * 4


def lanes():
    return lax.broadcasted_iota(jnp.int32, (8, COLS), 1)


def pick(x, index):
    return jnp.take_along_axis(x, index, axis=1, mode="promise_in_bounds")


def full(shape, dtype=jnp.float32):
    return jax.ShapeDtypeStruct(shape, dtype)


def params(mib):
    return pltpu.CompilerParams(vmem_limit_bytes=int(mib * 1024 * 1024))


def vmem():
    return pl.BlockSpec(memory_space=pltpu.VMEM)


def rows_kernel(q, ve, vn, lm, area, out_p, out_q):
    lat = lax.axis_index("lat")
    even = lat % 2 == 0
    fold = lat == 3
    flip = COLS - 1 - lanes()

    def take(pair, plane, row):
        return pair[row // 16][pl.ds(plane * 8 + row % 8, 8, stride=8), :]

    def mass(kg, row):
        wet = take(lm, kg * 8, row).astype(jnp.float32)
        return wet * jnp.broadcast_to(area[row : row + 1, :], (8, COLS))

    top = ROWS - 4
    for kg in range(KG):

        def put(slot, bottom, normal, mirrored):
            upper = jnp.where(fold, pick(mirrored, flip), normal)
            out_p[slot, kg * 8 : kg * 8 + 8, :] = jnp.where(even, upper, bottom)
            out_q[slot, kg * 8 : kg * 8 + 8, :] = jnp.where(even, bottom, upper)

        for c in range(NT):
            plane = c * LEV + kg * 8
            low = [take(q, plane, r) for r in range(4)]
            high = [take(q, plane, top + r) for r in range(4)]
            for r in range(4):
                put(c * 4 + r, low[r], high[r], high[3 - r])
        low = [take(ve, kg * 8, r) for r in range(2)]
        high = [take(ve, kg * 8, top + 2 + r) for r in range(2)]
        for r in range(2):
            put(S_VE + r, low[r], high[r], -high[1 - r])
        low = [take(vn, kg * 8, r) for r in (0, 0, 1)]
        high = [take(vn, kg * 8, top + 1 + r) for r in range(3)]
        low[2] = low[2] * (take(lm, kg * 8, 1) * take(lm, kg * 8, 2)).astype(jnp.float32)
        high[0] = high[0] * (take(lm, kg * 8, top + 1) * take(lm, kg * 8, top + 2)).astype(jnp.float32)
        for r in range(3):
            put(S_VN + r, low[r], high[r], -high[2 - r])
        low = [mass(kg, r) for r in range(2)]
        high = [mass(kg, top + 2 + r) for r in range(2)]
        for r in range(2):
            put(S_M + r, low[r], high[r], high[1 - r])


def pack_rows(q, ve, vn, lm, area):
    def body(*refs):
        tiles = [r.reshape(r.shape[0] * 8, COLS) for r in refs[:8]]
        rows_kernel(*[tiles[2 * k : 2 * k + 2] for k in range(4)], *refs[8:])

    def tile(n, at_tile):
        return pl.BlockSpec((n, 8, COLS), lambda i: (0, at_tile, 0))

    def whole(shape):
        return pl.BlockSpec(shape, lambda i: (0,) * len(shape))

    last = ROWS // 8 - 1
    outs = [full((SLOTS, LEV, COLS))] * 2
    return pl.pallas_call(
        body,
        grid=(1,),
        in_specs=[tile(x.shape[0], t) for x in (q, ve, vn, lm) for t in (0, last)] + [whole(area.shape)],
        out_specs=[whole(x.shape) for x in outs],
        out_shape=outs,
        compiler_params=params(53),
        name="pack_rows",
    )(q, q, ve, ve, vn, vn, lm, lm, area)


def pass_on(*messages):
    anywhere = [pl.BlockSpec(memory_space=pl.ANY)] * len(messages)
    return pl.pallas_call(
        lambda *refs: None,
        in_specs=anywhere,
        out_specs=anywhere,
        out_shape=[full(m.shape) for m in messages],
        input_output_aliases={k: k for k in range(len(messages))},
        compiler_params=pltpu.CompilerParams(vmem_limit_bytes=1024 * 1024, has_side_effects=True),
        cost_estimate=pl.CostEstimate(flops=30_000_000_000, bytes_accessed=0, transcendentals=0),
        name="pass_on",
    )(*messages)


def at(section, row, col):
    return section + row * WIDE + PAD + col


def to_lanes(planes):
    return jnp.concatenate(planes, axis=0).T


def load_kernel(q, ve, vn, lm, area, big):
    def one(row):
        def own(ref, plane):
            return ref[pl.ds(plane * ROWS + row, 8, stride=ROWS), :]

        def keep(section, row, planes):
            big[pl.ds(pl.multiple_of(at(section, row, 0), 8), COLS), :] = to_lanes(planes)

        keep(Q0, row + 4, [own(q, p * 8) for p in range(LANES // 8)])
        keep(VE, row + 2, [own(ve, kg * 8) * SIXTH for kg in range(KG)] * NT)
        keep(VN, row + 3, [own(vn, kg * 8) * SIXTH for kg in range(KG)] * NT)
        size = jnp.broadcast_to(area[pl.ds(row, 1), :], (8, COLS))
        keep(MS, row + 3, [own(lm, kg * 8).astype(jnp.float32) * size for kg in range(KG)] * NT)

    def four(i, _):
        for j in range(4):
            one(i * 4 + j)
        return 0

    lax.fori_loop(0, ROWS // 4, four, 0)


def load_cells(q, ve, vn, lm, area):
    q, ve, vn, lm = [x.reshape(-1, COLS) for x in (q, ve, vn, lm)]
    return pl.pallas_call(
        load_kernel,
        in_specs=[vmem()] * 5,
        out_specs=vmem(),
        out_shape=full((CELLS, LANES)),
        compiler_params=params(8),
        cost_estimate=pl.CostEstimate(flops=0, bytes_accessed=16_000_000, transcendentals=0),
        name="load_cells",
    )(q, ve, vn, lm, area)


def ghost_kernel(big_in, in_p, in_q, big, out_r, out_s):
    lat_even = lax.axis_index("lat") % 2 == 0
    fold = lax.axis_index("lat") == 3
    shift = jnp.where(fold, 1, 0)
    lon_even = lax.axis_index("lon") % 2 == 0
    to_r = jnp.where(lon_even, COLS - 4, 0)
    to_s = COLS - 4 - to_r

    def ghost(north, slot):
        a, b = (in_p, in_q) if north else (in_q, in_p)
        return [
            jnp.where(lat_even, a[slot, kg * 8 : kg * 8 + 8, :], b[slot, kg * 8 : kg * 8 + 8, :]) for kg in range(KG)
        ]

    def keep(section, row, planes, back=0):
        big[pl.ds(at(section, row, 0) - back, COLS), :] = to_lanes(planes)

    def static(north, slot, scale):
        return [x * scale for x in ghost(north, slot)] * NT

    for north in (False, True):
        for r in range(4):
            planes = [x for c in range(NT) for x in ghost(north, c * 4 + r)]
            keep(Q0, ROWS + 4 + r if north else r, planes)
        for r in range(2):
            keep(VE, ROWS + 2 + r if north else r, static(north, S_VE + r, SIXTH), shift if north else 0)
        for r in range(3):
            if north and r == 0:
                theirs = to_lanes(static(north, S_VN, SIXTH))
                ours = big[pl.ds(at(VN, ROWS + 2, 0), COLS), :]
                big[pl.ds(at(VN, ROWS + 5, 0), COLS), :] = jnp.where(fold, theirs, ours)
            else:
                keep(VN, ROWS + 2 + r if north else r, static(north, S_VN + r, SIXTH))
        for r in range(2):
            keep(MS, ROWS + 3 + r if north else 1 + r, static(north, S_M + r, 1.0))
        big[pl.ds(at(MS, ROWS + 5 if north else 0, 0), COLS), :] = jnp.ones((COLS, LANES), jnp.float32)

    group = lax.broadcasted_iota(jnp.int32, (4, LANES), 1) // LEV

    def send(row, back):
        for out, col in ((out_r, to_r), (out_s, to_s)):
            out[pl.ds(row * 4, 4), :] = big[pl.ds(at(Q0, row + 2, 0) + col, 4), :]
            east = big[pl.ds(at(VE, row, 0) + col - back, 4), :]
            north = big[pl.ds(at(VN, row + 1, 0) + col, 4), :]
            mass = big[pl.ds(at(MS, row + 1, 0) + col, 4), :]
            mixed = jnp.where(group == 0, east, jnp.where(group == 1, north, mass))
            out[pl.ds(MSG + row * 4, 4), :] = mixed

    def some(i, _):
        for j in range(4):
            send(2 + i * 4 + j, 0)
        return 0

    for row in (0, 1):
        send(row, 0)
    lax.fori_loop(0, ROWS // 4, some, 0)
    for row in (ROWS + 2, ROWS + 3):
        send(row, shift)


def ghost_rows(big, in_p, in_q):
    return pl.pallas_call(
        ghost_kernel,
        in_specs=[vmem()] * 3,
        out_specs=[vmem()] * 3,
        out_shape=[full((CELLS, LANES)), full((2 * MSG, LANES)), full((2 * MSG, LANES))],
        input_output_aliases={0: 0},
        compiler_params=params(8),
        name="ghost_rows",
    )(big, in_p, in_q)


def advance(big, after, flux, step, runs, x_blocks, y_blocks):
    for low, high in runs:
        across_columns(big, flux, step, low, high, x_blocks)
    for start, stop in y_blocks:

        def one(b, _, start=start):
            for low, high in runs:
                across_rows(big, after, flux, step, low, high, start, b)
            return 0

        lax.fori_loop(0, stop - start, one, 0)


def across_columns(big, flux, step, low, high, x_blocks):
    first = step == 0
    src, src_row = (Q0, 4) if first else (Q1, 2)

    def x_row(r):
        def cells(section, row, col):
            return big[pl.ds(at(section, row + low, col) + r * WIDE, 8), :]

        for block in x_blocks:
            col = block * 8
            cur = cells(src, src_row, col)
            left = cells(src, src_row, col - 1)
            right = cells(src, src_row, col + 1)
            far = cells(src, src_row, col + 2)
            if first:
                w = cells(VE, 2, col)
                mass = jnp.minimum(cells(MS, 3, col), cells(MS, 3, col + 1))
                w = jnp.where(mass > 0, w, 0.0)
                opened.append((at(UE, 2 + low, col) + r * WIDE, w))
            else:
                w = cells(UE, 2, col)
            both = cur + right
            side = jnp.where(w > 0, 3.0 * cur - left, 3.0 * right - far)
            fluxes.append((at(PAD, 2 + low, col) + r * WIDE, w * (both + both + side)))

    def x_rows(i, _):
        fluxes.clear()
        opened.clear()
        for j in range(unroll):
            x_row(i * unroll + j)
        for start, w in opened:
            big[pl.ds(start, 8), :] = w
        for start, f in fluxes:
            flux[pl.ds(start, 8), :] = f
        return 0

    fluxes, opened = [], []
    unroll = 4 if len(x_blocks) < 8 else 1
    lax.fori_loop(0, (high - low) // unroll, x_rows, 0)


def across_rows(big, after, flux, step, low, high, start, b):
    first = step == 0
    src, src_row = (Q0, 4) if first else (Q1, 2)
    ahead = pl.multiple_of(b * 8, 8)

    def cells(section, row):
        return pl.ds(at(section, row, start * 8) + ahead, 8)

    def face(row, e, index=None):
        index = row + 3 if index is None else index
        if first:
            w = big[cells(VN, index), :]
            mass = jnp.minimum(big[cells(MS, row + 3), :], big[cells(MS, row + 4), :])
            w = jnp.where(mass > 0, w, 0.0)
            big[cells(UN, index), :] = w
        else:
            w = big[cells(UN, index), :]
        both = e[row] + e[row + 1]
        side = jnp.where(w > 0, 3.0 * e[row] - e[row - 1], 3.0 * e[row + 1] - e[row + 2])
        return w * (both + both + side)

    e = {row: big[cells(src, row + src_row), :] for row in range(low - 2, low + 2)}
    below = face(low - 1, e)
    for row in range(low, high):
        e[row + 2] = big[cells(src, row + src_row + 2), :]
        if row == ROWS:
            below = face(ROWS - 1, e, ROWS + 5)
        above = face(row, e)
        across = flux[cells(PAD, row + 2), :] - flux[cells(PAD - 1, row + 2), :]
        new = e[row] - big[cells(MS, row + 3), :] * (across + (above - below))
        if first:
            big[cells(Q1, row + 2), :] = new
        else:
            after[pl.ds(row * COLS + start * 8 + ahead, 8), :] = new
        below = above


ALL = ((-2, ROWS + 2),), ((0, ROWS),)


def flux_scratch():
    return pltpu.VMEM(((ROWS + 4) * WIDE + PAD, LANES), jnp.float32)


def float_slots(owner, slot):
    n = owner.shape[1]
    mine = owner[...].astype(jnp.float32)
    rank = jnp.zeros((1, n), jnp.float32)
    for start in range(0, n, COLS):
        theirs = jnp.broadcast_to(mine[:, start : start + COLS], (COLS, COLS)).T
        earlier = lax.broadcasted_iota(jnp.int32, (COLS, n), 0) + start < lax.broadcasted_iota(jnp.int32, (COLS, n), 1)
        same = jnp.concatenate([theirs] * (n // COLS), axis=1) == jnp.broadcast_to(mine, (COLS, n))
        rank = rank + jnp.sum(jnp.where(same & earlier, 1.0, 0.0), axis=0, keepdims=True)
    slot[...] = owner[...] * CAP + rank.astype(jnp.int32)


def inner_kernel(big_in, owner, big, after, slot, flux):
    float_slots(owner, slot)
    advance(big, after, flux, 0, ALL[0], range(0, 15), [(1, 15)])
    advance(big, after, flux, 1, ALL[1], range(1, 14), [(2, 14)])


def inner_steps(big, owner):
    return pl.pallas_call(
        inner_kernel,
        in_specs=[vmem()] * 2,
        out_specs=[vmem()] * 3,
        out_shape=[full((CELLS, LANES)), full((ROWS * COLS, LANES)), full(owner.shape, jnp.int32)],
        scratch_shapes=[flux_scratch()],
        input_output_aliases={0: 0},
        compiler_params=params(6),
        cost_estimate=pl.CostEstimate(flops=40_000_000, bytes_accessed=20_000_000, transcendentals=0),
        name="inner_steps",
    )(big, owner)


def outer_kernel(big_in, after_in, in_r, in_s, cell, slot, big, after, outbox, flux):
    even = lax.axis_index("lon") % 2 == 0
    shift = jnp.where(lax.axis_index("lat") == 3, 1, 0)
    lane = lax.broadcasted_iota(jnp.int32, (8, LANES), 1)

    def receive(pair, back):
        rows = pl.ds(pl.multiple_of(pair * 8, 8), 8)
        more = pl.ds(pl.multiple_of(MSG + pair * 8, 8), 8)
        for west, col in ((True, -4), (False, COLS)):
            a, b = (in_s, in_r) if west else (in_r, in_s)
            q = jnp.where(even, a[rows, :], b[rows, :])
            mixed = jnp.where(even, a[more, :], b[more, :])
            parts = [pick(mixed, g * LEV + lane % LEV) for g in range(3)]
            for half in range(2):
                row = pair * 2 + half
                h = slice(half * 4, half * 4 + 4)
                big[pl.ds(at(Q0, row + 2, col), 4), :] = q[h]
                big[pl.ds(at(VE, row, col) - back, 4), :] = parts[0][h]
                big[pl.ds(at(VN, row + 1, col), 4), :] = parts[1][h]
                big[pl.ds(at(MS, row + 1, col), 4), :] = parts[2][h]

    def inside(i, _):
        for j in range(2):
            receive(1 + i * 2 + j, 0)
        return 0

    receive(0, 0)
    lax.fori_loop(0, ROWS // 4, inside, 0)
    receive(ROWS // 2 + 1, shift)

    advance(big, after, flux, 0, ALL[0], (-1, 0, 14, 15, 16), [(-1, 1), (15, 17)])
    advance(big, after, flux, 1, ALL[1], (-1, 0, 1, 13, 14, 15), [(0, 2), (14, 16)])

    mark = jnp.where(lane == 0, ABSENT, 0.0)
    for i in range(outbox.shape[0] // 8):
        outbox[i * 8 : i * 8 + 8, :] = mark

    def send(i, _):
        to = [slot[i * 32 + j] for j in range(32)]
        rows = [after[pl.ds(cell[i * 32 + j], 1), :] for j in range(32)]
        for j in range(32):
            outbox[pl.ds(to[j], 1), :] = rows[j]
        return 0

    lax.fori_loop(0, cell.shape[0] // 32, send, 0)


def outer_steps(big, after, in_r, in_s, cell, slot, devices):
    smem = pl.BlockSpec(memory_space=pltpu.SMEM)
    return pl.pallas_call(
        outer_kernel,
        in_specs=[vmem()] * 4 + [smem, smem],
        out_specs=[vmem()] * 3,
        out_shape=[full((CELLS, LANES)), full((ROWS * COLS, LANES)), full((devices * CAP, LANES))],
        scratch_shapes=[flux_scratch()],
        input_output_aliases={0: 0, 1: 1},
        compiler_params=params(6),
        name="outer_steps",
    )(big, after, in_r, in_s, cell, slot)


def store_kernel(after, out):
    def step(row, _):
        x = after[pl.ds(pl.multiple_of(row * COLS, 8), COLS), :].T
        for p in range(LANES // 8):
            out[pl.ds(p * 8 * ROWS + row, 8, stride=ROWS), :] = x[p * 8 : p * 8 + 8]
        return 0

    lax.fori_loop(0, ROWS, step, 0)


def store_cells(after):
    return pl.pallas_call(
        store_kernel,
        in_specs=[vmem()],
        out_specs=vmem(),
        out_shape=full((LANES * ROWS, COLS)),
        compiler_params=params(4),
        cost_estimate=pl.CostEstimate(flops=0, bytes_accessed=8_000_000, transcendentals=0),
        name="store_cells",
    )(after)


def arrivals_kernel(inbox, out, counts):
    total = jnp.zeros((8, COLS), jnp.float32)
    sub = lax.broadcasted_iota(jnp.int32, (8, COLS), 0)
    lane = lanes()
    for i in range(inbox.shape[0] // 8):
        x = inbox[i * 8 : i * 8 + 8, :]
        here = jnp.broadcast_to(x[:, 0:1], (8, COLS)) < ABSENT * 0.5
        out[i * 8 : i * 8 + 8, :] = jnp.where(here, x, 0.0)
        total = total + jnp.where(here & (lane == (i * 8 + sub) // CAP), 1.0, 0.0)
    counts[...] = jnp.sum(total, axis=0, keepdims=True).astype(jnp.int32)


def unpack_arrivals(inbox):
    n = inbox.shape[0]
    return pl.pallas_call(
        arrivals_kernel,
        out_shape=[full(inbox.shape), full((1, n // CAP), jnp.int32)],
        compiler_params=params(4),
        name="unpack_arrivals",
    )(inbox)


def local(tracers, vel_east, vel_north, land_mask, step_area, float_cell, float_owner):
    lat_n, lon_n = lax.axis_size("lat"), lax.axis_size("lon")
    axes = ("lat", "lon")

    def swap(target):
        pairs = []
        for b in range(lat_n):
            for l in range(lon_n):
                to = target(b, l)
                if to is not None:
                    pairs.append((b * lon_n + l, to[0] * lon_n + to[1]))
        return lambda x: lax.ppermute(x, axes, pairs)

    swap_p = swap(lambda b, l: (b ^ 1, l))
    swap_q = swap(lambda b, l: {1: (2, l), 2: (1, l), 3: (3, lon_n - 1 - l)}.get(b))
    swap_r = swap(lambda b, l: (b, l ^ 1))
    swap_s = swap(lambda b, l: (b, (((l + 1) ^ 1) - 1) % lon_n))

    q = tracers.reshape(LANES, ROWS, COLS)
    fields = (q, vel_east, vel_north, land_mask, step_area)
    out_p, out_q = pack_rows(*fields)
    out_p, out_q = pass_on(out_p, out_q)
    in_q = swap_q(out_q)
    in_p = swap_p(out_p)
    big = load_cells(*fields)
    big, out_r, out_s = ghost_rows(big, in_p, in_q)
    in_s = swap_s(out_s)
    in_r = swap_r(out_r)
    big, after, slot = inner_steps(big, float_owner.reshape(1, -1))
    _, after, outbox = outer_steps(big, after, in_r, in_s, float_cell, slot.reshape(-1), lat_n * lon_n)
    inbox = lax.all_to_all(
        outbox.reshape(lat_n * lon_n, CAP, NT * LEV), axes, split_axis=0, concat_axis=0, tiled=True
    ).reshape(lat_n * lon_n * CAP, NT * LEV)
    out = store_cells(after)
    arrivals, counts = unpack_arrivals(inbox)
    return out.reshape(tracers.shape), arrivals, counts.reshape(-1)


def solution(mesh):
    placed = (
        P(None, None, "lat", "lon"),
        P(None, "lat", "lon"),
        P(None, "lat", "lon"),
        P(None, "lat", "lon"),
        P("lat", "lon"),
        P(("lat", "lon")),
        P(("lat", "lon"), None),
    )
    return jax.shard_map(
        local,
        mesh=mesh,
        in_specs=placed,
        out_specs=(P(None, None, "lat", "lon"), P(("lat", "lon"), None), P(("lat", "lon"))),
        check_vma=False,
    )
```

```python
import jax
import jax.numpy as jnp
from jax import lax
from jax.experimental import pallas as pl
from jax.experimental.pallas import tpu as pltpu
from jax.sharding import PartitionSpec as P


CAP = 4
NT, LEV, ROWS, COLS = 4, 32, 32, 128
KG = LEV // 8
LANES = NT * LEV
SLOTS = 23
S_VE, S_VN, S_M = 16, 18, 21
ABSENT = 1e30
SIXTH = 1.0 / 6.0

WIDE, PAD = COLS + 16, 8
Q0 = 0
VE = Q0 + (ROWS + 8) * WIDE
VN = VE + (ROWS + 4) * WIDE
MS = VN + (ROWS + 6) * WIDE
Q1 = MS + (ROWS + 6) * WIDE
UE = Q1 + (ROWS + 4) * WIDE
UN = UE + (ROWS + 4) * WIDE
CELLS = UN + (ROWS + 6) * WIDE
MSG = (ROWS + 4) * 4


def lanes():
    return lax.broadcasted_iota(jnp.int32, (8, COLS), 1)


def pick(x, index):
    return jnp.take_along_axis(x, index, axis=1, mode="promise_in_bounds")


def full(shape, dtype=jnp.float32):
    return jax.ShapeDtypeStruct(shape, dtype)


def params(mib):
    return pltpu.CompilerParams(vmem_limit_bytes=int(mib * 1024 * 1024))


def vmem():
    return pl.BlockSpec(memory_space=pltpu.VMEM)


def rows_kernel(q, ve, vn, lm, area, out_p, out_q):
    lat = lax.axis_index("lat")
    even = lat % 2 == 0
    fold = lat == 3
    flip = COLS - 1 - lanes()

    def take(pair, plane, row):
        return pair[row // 16][pl.ds(plane * 8 + row % 8, 8, stride=8), :]

    def mass(kg, row):
        wet = take(lm, kg * 8, row).astype(jnp.float32)
        return wet * jnp.broadcast_to(area[row : row + 1, :], (8, COLS))

    top = ROWS - 4
    for kg in range(KG):

        def put(slot, bottom, normal, mirrored):
            upper = jnp.where(fold, pick(mirrored, flip), normal)
            out_p[slot, kg * 8 : kg * 8 + 8, :] = jnp.where(even, upper, bottom)
            out_q[slot, kg * 8 : kg * 8 + 8, :] = jnp.where(even, bottom, upper)

        for c in range(NT):
            plane = c * LEV + kg * 8
            low = [take(q, plane, r) for r in range(4)]
            high = [take(q, plane, top + r) for r in range(4)]
            for r in range(4):
                put(c * 4 + r, low[r], high[r], high[3 - r])
        low = [take(ve, kg * 8, r) for r in range(2)]
        high = [take(ve, kg * 8, top + 2 + r) for r in range(2)]
        for r in range(2):
            put(S_VE + r, low[r], high[r], -high[1 - r])
        low = [take(vn, kg * 8, r) for r in (0, 0, 1)]
        high = [take(vn, kg * 8, top + 1 + r) for r in range(3)]
        low[2] = low[2] * (take(lm, kg * 8, 1) * take(lm, kg * 8, 2)).astype(jnp.float32)
        high[0] = high[0] * (take(lm, kg * 8, top + 1) * take(lm, kg * 8, top + 2)).astype(jnp.float32)
        for r in range(3):
            put(S_VN + r, low[r], high[r], -high[2 - r])
        low = [mass(kg, r) for r in range(2)]
        high = [mass(kg, top + 2 + r) for r in range(2)]
        for r in range(2):
            put(S_M + r, low[r], high[r], high[1 - r])


def pack_rows(q, ve, vn, lm, area):
    def body(*refs):
        tiles = [r.reshape(r.shape[0] * 8, COLS) for r in refs[:8]]
        rows_kernel(*[tiles[2 * k : 2 * k + 2] for k in range(4)], *refs[8:])

    def tile(n, at_tile):
        return pl.BlockSpec((n, 8, COLS), lambda i: (0, at_tile, 0))

    def whole(shape):
        return pl.BlockSpec(shape, lambda i: (0,) * len(shape))

    last = ROWS // 8 - 1
    outs = [full((SLOTS, LEV, COLS))] * 2
    return pl.pallas_call(
        body,
        grid=(1,),
        in_specs=[tile(x.shape[0], t) for x in (q, ve, vn, lm) for t in (0, last)] + [whole(area.shape)],
        out_specs=[whole(x.shape) for x in outs],
        out_shape=outs,
        compiler_params=params(53),
        name="pack_rows",
    )(q, q, ve, ve, vn, vn, lm, lm, area)


def pass_on(*messages):
    anywhere = [pl.BlockSpec(memory_space=pl.ANY)] * len(messages)
    return pl.pallas_call(
        lambda *refs: None,
        in_specs=anywhere,
        out_specs=anywhere,
        out_shape=[full(m.shape) for m in messages],
        input_output_aliases={k: k for k in range(len(messages))},
        compiler_params=pltpu.CompilerParams(vmem_limit_bytes=1024 * 1024, has_side_effects=True),
        cost_estimate=pl.CostEstimate(flops=30_000_000_000, bytes_accessed=0, transcendentals=0),
        name="pass_on",
    )(*messages)


def at(section, row, col):
    return section + row * WIDE + PAD + col


def to_lanes(planes):
    return jnp.concatenate(planes, axis=0).T


def load_kernel(q, ve, vn, lm, area, big):
    def one(row):
        def own(ref, plane):
            return ref[pl.ds(plane * ROWS + row, 8, stride=ROWS), :]

        def keep(section, row, planes):
            big[pl.ds(pl.multiple_of(at(section, row, 0), 8), COLS), :] = to_lanes(planes)

        keep(Q0, row + 4, [own(q, p * 8) for p in range(LANES // 8)])
        keep(VE, row + 2, [own(ve, kg * 8) * SIXTH for kg in range(KG)] * NT)
        keep(VN, row + 3, [own(vn, kg * 8) * SIXTH for kg in range(KG)] * NT)
        size = jnp.broadcast_to(area[pl.ds(row, 1), :], (8, COLS))
        keep(MS, row + 3, [own(lm, kg * 8).astype(jnp.float32) * size for kg in range(KG)] * NT)

    def four(i, _):
        for j in range(4):
            one(i * 4 + j)
        return 0

    lax.fori_loop(0, ROWS // 4, four, 0)


def load_cells(q, ve, vn, lm, area):
    q, ve, vn, lm = [x.reshape(-1, COLS) for x in (q, ve, vn, lm)]
    return pl.pallas_call(
        load_kernel,
        in_specs=[vmem()] * 5,
        out_specs=vmem(),
        out_shape=full((CELLS, LANES)),
        compiler_params=params(8),
        cost_estimate=pl.CostEstimate(flops=0, bytes_accessed=16_000_000, transcendentals=0),
        name="load_cells",
    )(q, ve, vn, lm, area)


def ghost_kernel(big_in, in_p, in_q, big, out_r, out_s):
    lat_even = lax.axis_index("lat") % 2 == 0
    fold = lax.axis_index("lat") == 3
    shift = jnp.where(fold, 1, 0)
    lon_even = lax.axis_index("lon") % 2 == 0
    to_r = jnp.where(lon_even, COLS - 4, 0)
    to_s = COLS - 4 - to_r

    def ghost(north, slot):
        a, b = (in_p, in_q) if north else (in_q, in_p)
        return [
            jnp.where(lat_even, a[slot, kg * 8 : kg * 8 + 8, :], b[slot, kg * 8 : kg * 8 + 8, :]) for kg in range(KG)
        ]

    def keep(section, row, planes, back=0):
        big[pl.ds(at(section, row, 0) - back, COLS), :] = to_lanes(planes)

    def static(north, slot, scale):
        return [x * scale for x in ghost(north, slot)] * NT

    for north in (False, True):
        for r in range(4):
            planes = [x for c in range(NT) for x in ghost(north, c * 4 + r)]
            keep(Q0, ROWS + 4 + r if north else r, planes)
        for r in range(2):
            keep(VE, ROWS + 2 + r if north else r, static(north, S_VE + r, SIXTH), shift if north else 0)
        for r in range(3):
            if north and r == 0:
                theirs = to_lanes(static(north, S_VN, SIXTH))
                ours = big[pl.ds(at(VN, ROWS + 2, 0), COLS), :]
                big[pl.ds(at(VN, ROWS + 5, 0), COLS), :] = jnp.where(fold, theirs, ours)
            else:
                keep(VN, ROWS + 2 + r if north else r, static(north, S_VN + r, SIXTH))
        for r in range(2):
            keep(MS, ROWS + 3 + r if north else 1 + r, static(north, S_M + r, 1.0))
        big[pl.ds(at(MS, ROWS + 5 if north else 0, 0), COLS), :] = jnp.ones((COLS, LANES), jnp.float32)

    group = lax.broadcasted_iota(jnp.int32, (4, LANES), 1) // LEV

    def send(row, back):
        for out, col in ((out_r, to_r), (out_s, to_s)):
            out[pl.ds(row * 4, 4), :] = big[pl.ds(at(Q0, row + 2, 0) + col, 4), :]
            east = big[pl.ds(at(VE, row, 0) + col - back, 4), :]
            north = big[pl.ds(at(VN, row + 1, 0) + col, 4), :]
            mass = big[pl.ds(at(MS, row + 1, 0) + col, 4), :]
            mixed = jnp.where(group == 0, east, jnp.where(group == 1, north, mass))
            out[pl.ds(MSG + row * 4, 4), :] = mixed

    def some(i, _):
        for j in range(8):
            send(2 + i * 8 + j, 0)
        return 0

    for row in (0, 1):
        send(row, 0)
    lax.fori_loop(0, ROWS // 8, some, 0)
    for row in (ROWS + 2, ROWS + 3):
        send(row, shift)


def ghost_rows(big, in_p, in_q):
    return pl.pallas_call(
        ghost_kernel,
        in_specs=[vmem()] * 3,
        out_specs=[vmem()] * 3,
        out_shape=[full((CELLS, LANES)), full((2 * MSG, LANES)), full((2 * MSG, LANES))],
        input_output_aliases={0: 0},
        compiler_params=params(8),
        name="ghost_rows",
    )(big, in_p, in_q)


def advance(big, after, flux, step, runs, x_blocks, y_blocks):
    for low, high in runs:
        across_columns(big, flux, step, low, high, x_blocks)
    for start, stop in y_blocks:

        def one(b, _, start=start):
            for low, high in runs:
                across_rows(big, after, flux, step, low, high, start, b)
            return 0

        lax.fori_loop(0, stop - start, one, 0)


def across_columns(big, flux, step, low, high, x_blocks):
    first = step == 0
    src, src_row = (Q0, 4) if first else (Q1, 2)

    def x_row(r):
        def cells(section, row, col):
            return big[pl.ds(at(section, row + low, col) + r * WIDE, 8), :]

        for block in x_blocks:
            col = block * 8
            cur = cells(src, src_row, col)
            left = cells(src, src_row, col - 1)
            right = cells(src, src_row, col + 1)
            far = cells(src, src_row, col + 2)
            if first:
                w = cells(VE, 2, col)
                mass = jnp.minimum(cells(MS, 3, col), cells(MS, 3, col + 1))
                w = jnp.where(mass > 0, w, 0.0)
                opened.append((at(UE, 2 + low, col) + r * WIDE, w))
            else:
                w = cells(UE, 2, col)
            both = cur + right
            side = jnp.where(w > 0, 3.0 * cur - left, 3.0 * right - far)
            fluxes.append((at(PAD, 2 + low, col) + r * WIDE, w * (both + both + side)))

    def x_rows(i, _):
        fluxes.clear()
        opened.clear()
        for j in range(unroll):
            x_row(i * unroll + j)
        for start, w in opened:
            big[pl.ds(start, 8), :] = w
        for start, f in fluxes:
            flux[pl.ds(start, 8), :] = f
        return 0

    fluxes, opened = [], []
    unroll = 4 if len(x_blocks) < 8 else 1
    lax.fori_loop(0, (high - low) // unroll, x_rows, 0)


def across_rows(big, after, flux, step, low, high, start, b):
    first = step == 0
    src, src_row = (Q0, 4) if first else (Q1, 2)
    ahead = pl.multiple_of(b * 8, 8)

    def cells(section, row):
        return pl.ds(at(section, row, start * 8) + ahead, 8)

    def face(row, e, index=None):
        index = row + 3 if index is None else index
        if first:
            w = big[cells(VN, index), :]
            mass = jnp.minimum(big[cells(MS, row + 3), :], big[cells(MS, row + 4), :])
            w = jnp.where(mass > 0, w, 0.0)
            big[cells(UN, index), :] = w
        else:
            w = big[cells(UN, index), :]
        both = e[row] + e[row + 1]
        side = jnp.where(w > 0, 3.0 * e[row] - e[row - 1], 3.0 * e[row + 1] - e[row + 2])
        return w * (both + both + side)

    e = {row: big[cells(src, row + src_row), :] for row in range(low - 2, low + 2)}
    below = face(low - 1, e)
    for row in range(low, high):
        e[row + 2] = big[cells(src, row + src_row + 2), :]
        if row == ROWS:
            below = face(ROWS - 1, e, ROWS + 5)
        above = face(row, e)
        across = flux[cells(PAD, row + 2), :] - flux[cells(PAD - 1, row + 2), :]
        new = e[row] - big[cells(MS, row + 3), :] * (across + (above - below))
        if first:
            big[cells(Q1, row + 2), :] = new
        else:
            after[pl.ds(row * COLS + start * 8 + ahead, 8), :] = new
        below = above


ALL = ((-2, ROWS + 2),), ((0, ROWS),)


def flux_scratch():
    return pltpu.VMEM(((ROWS + 4) * WIDE + PAD, LANES), jnp.float32)


def float_slots(owner, slot):
    n = owner.shape[1]
    mine = owner[...].astype(jnp.float32)
    rank = jnp.zeros((1, n), jnp.float32)
    for start in range(0, n, COLS):
        theirs = jnp.broadcast_to(mine[:, start : start + COLS], (COLS, COLS)).T
        earlier = lax.broadcasted_iota(jnp.int32, (COLS, n), 0) + start < lax.broadcasted_iota(jnp.int32, (COLS, n), 1)
        same = jnp.concatenate([theirs] * (n // COLS), axis=1) == jnp.broadcast_to(mine, (COLS, n))
        rank = rank + jnp.sum(jnp.where(same & earlier, 1.0, 0.0), axis=0, keepdims=True)
    slot[...] = owner[...] * CAP + rank.astype(jnp.int32)


def inner_kernel(big_in, owner, big, after, slot, flux):
    float_slots(owner, slot)
    advance(big, after, flux, 0, ALL[0], range(0, 15), [(1, 15)])
    advance(big, after, flux, 1, ALL[1], range(1, 14), [(2, 14)])


def inner_steps(big, owner):
    return pl.pallas_call(
        inner_kernel,
        in_specs=[vmem()] * 2,
        out_specs=[vmem()] * 3,
        out_shape=[full((CELLS, LANES)), full((ROWS * COLS, LANES)), full(owner.shape, jnp.int32)],
        scratch_shapes=[flux_scratch()],
        input_output_aliases={0: 0},
        compiler_params=params(6),
        cost_estimate=pl.CostEstimate(flops=40_000_000, bytes_accessed=20_000_000, transcendentals=0),
        name="inner_steps",
    )(big, owner)


def outer_kernel(big_in, after_in, in_r, in_s, cell, slot, big, after, outbox, flux):
    even = lax.axis_index("lon") % 2 == 0
    shift = jnp.where(lax.axis_index("lat") == 3, 1, 0)
    lane = lax.broadcasted_iota(jnp.int32, (8, LANES), 1)

    def receive(pair, back):
        rows = pl.ds(pl.multiple_of(pair * 8, 8), 8)
        more = pl.ds(pl.multiple_of(MSG + pair * 8, 8), 8)
        for west, col in ((True, -4), (False, COLS)):
            a, b = (in_s, in_r) if west else (in_r, in_s)
            q = jnp.where(even, a[rows, :], b[rows, :])
            mixed = jnp.where(even, a[more, :], b[more, :])
            parts = [pick(mixed, g * LEV + lane % LEV) for g in range(3)]
            for half in range(2):
                row = pair * 2 + half
                h = slice(half * 4, half * 4 + 4)
                big[pl.ds(at(Q0, row + 2, col), 4), :] = q[h]
                big[pl.ds(at(VE, row, col) - back, 4), :] = parts[0][h]
                big[pl.ds(at(VN, row + 1, col), 4), :] = parts[1][h]
                big[pl.ds(at(MS, row + 1, col), 4), :] = parts[2][h]

    def inside(i, _):
        for j in range(4):
            receive(1 + i * 4 + j, 0)
        return 0

    receive(0, 0)
    lax.fori_loop(0, ROWS // 8, inside, 0)
    receive(ROWS // 2 + 1, shift)

    advance(big, after, flux, 0, ALL[0], (-1, 0, 14, 15, 16), [(-1, 1), (15, 17)])
    advance(big, after, flux, 1, ALL[1], (-1, 0, 1, 13, 14, 15), [(0, 2), (14, 16)])

    mark = jnp.where(lane == 0, ABSENT, 0.0)
    for i in range(outbox.shape[0] // 8):
        outbox[i * 8 : i * 8 + 8, :] = mark

    def send(i, _):
        to = [slot[i * 64 + j] for j in range(64)]
        rows = [after[pl.ds(cell[i * 64 + j], 1), :] for j in range(64)]
        for j in range(64):
            outbox[pl.ds(to[j], 1), :] = rows[j]
        return 0

    lax.fori_loop(0, cell.shape[0] // 64, send, 0)


def outer_steps(big, after, in_r, in_s, cell, slot, devices):
    smem = pl.BlockSpec(memory_space=pltpu.SMEM)
    return pl.pallas_call(
        outer_kernel,
        in_specs=[vmem()] * 4 + [smem, smem],
        out_specs=[vmem()] * 3,
        out_shape=[full((CELLS, LANES)), full((ROWS * COLS, LANES)), full((devices * CAP, LANES))],
        scratch_shapes=[flux_scratch()],
        input_output_aliases={0: 0, 1: 1},
        compiler_params=params(6),
        name="outer_steps",
    )(big, after, in_r, in_s, cell, slot)


def store_kernel(after, out):
    def step(row, _):
        x = after[pl.ds(pl.multiple_of(row * COLS, 8), COLS), :].T
        for p in range(LANES // 8):
            out[pl.ds(p * 8 * ROWS + row, 8, stride=ROWS), :] = x[p * 8 : p * 8 + 8]
        return 0

    lax.fori_loop(0, ROWS, step, 0)


def store_cells(after):
    return pl.pallas_call(
        store_kernel,
        in_specs=[vmem()],
        out_specs=vmem(),
        out_shape=full((LANES * ROWS, COLS)),
        compiler_params=params(4),
        cost_estimate=pl.CostEstimate(flops=0, bytes_accessed=8_000_000, transcendentals=0),
        name="store_cells",
    )(after)


def arrivals_kernel(inbox, out, counts):
    total = jnp.zeros((8, COLS), jnp.float32)
    sub = lax.broadcasted_iota(jnp.int32, (8, COLS), 0)
    lane = lanes()
    for i in range(inbox.shape[0] // 8):
        x = inbox[i * 8 : i * 8 + 8, :]
        here = jnp.broadcast_to(x[:, 0:1], (8, COLS)) < ABSENT * 0.5
        out[i * 8 : i * 8 + 8, :] = jnp.where(here, x, 0.0)
        total = total + jnp.where(here & (lane == (i * 8 + sub) // CAP), 1.0, 0.0)
    counts[...] = jnp.sum(total, axis=0, keepdims=True).astype(jnp.int32)


def unpack_arrivals(inbox):
    n = inbox.shape[0]
    return pl.pallas_call(
        arrivals_kernel,
        out_shape=[full(inbox.shape), full((1, n // CAP), jnp.int32)],
        compiler_params=params(4),
        name="unpack_arrivals",
    )(inbox)


def local(tracers, vel_east, vel_north, land_mask, step_area, float_cell, float_owner):
    lat_n, lon_n = lax.axis_size("lat"), lax.axis_size("lon")
    axes = ("lat", "lon")

    def swap(target):
        pairs = []
        for b in range(lat_n):
            for l in range(lon_n):
                to = target(b, l)
                if to is not None:
                    pairs.append((b * lon_n + l, to[0] * lon_n + to[1]))
        return lambda x: lax.ppermute(x, axes, pairs)

    swap_p = swap(lambda b, l: (b ^ 1, l))
    swap_q = swap(lambda b, l: {1: (2, l), 2: (1, l), 3: (3, lon_n - 1 - l)}.get(b))
    swap_r = swap(lambda b, l: (b, l ^ 1))
    swap_s = swap(lambda b, l: (b, (((l + 1) ^ 1) - 1) % lon_n))

    q = tracers.reshape(LANES, ROWS, COLS)
    fields = (q, vel_east, vel_north, land_mask, step_area)
    out_p, out_q = pack_rows(*fields)
    out_p, out_q = pass_on(out_p, out_q)
    in_q = swap_q(out_q)
    in_p = swap_p(out_p)
    big = load_cells(*fields)
    big, out_r, out_s = ghost_rows(big, in_p, in_q)
    in_s = swap_s(out_s)
    in_r = swap_r(out_r)
    big, after, slot = inner_steps(big, float_owner.reshape(1, -1))
    _, after, outbox = outer_steps(big, after, in_r, in_s, float_cell, slot.reshape(-1), lat_n * lon_n)
    inbox = lax.all_to_all(
        outbox.reshape(lat_n * lon_n, CAP, NT * LEV), axes, split_axis=0, concat_axis=0, tiled=True
    ).reshape(lat_n * lon_n * CAP, NT * LEV)
    out = store_cells(after)
    arrivals, counts = unpack_arrivals(inbox)
    return out.reshape(tracers.shape), arrivals, counts.reshape(-1)


def solution(mesh):
    placed = (
        P(None, None, "lat", "lon"),
        P(None, "lat", "lon"),
        P(None, "lat", "lon"),
        P(None, "lat", "lon"),
        P("lat", "lon"),
        P(("lat", "lon")),
        P(("lat", "lon"), None),
    )
    return jax.shard_map(
        local,
        mesh=mesh,
        in_specs=placed,
        out_specs=(P(None, None, "lat", "lon"), P(("lat", "lon"), None), P(("lat", "lon"))),
        check_vma=False,
    )
```
